128 devices in a mesh: seq: 32 (over x, y, core), exp: 4 (over z).
Axes of the slice: x: 4, y: 4, z: 4, core: 2. Of those that a mesh axis runs over, the one named last changes fastest.
Arguments:
- residual_in: bfloat16 [8192, 3072], P('seq'), may hold values from -6 to 6
- queries: bfloat16 [8192, 4096], P('seq', 'exp'), may hold values from -6 to 6
- keys: bfloat16 [8192, 4096], P('seq', 'exp'), may hold values from -6 to 6
- values: bfloat16 [8192, 4096], P('seq', 'exp'), may hold values from -6 to 6
- rates: float32 [32], P('exp'), may hold values from 7.6293945e-06 to 0.0333333333, as said below
- doc_lengths: int32 [16], replicated, may hold values from 1 to 4096, 8192 in all
- out_weight: bfloat16 [4096, 3072], P('exp'), may hold values from -0.09375 to 0.09375
- router: bfloat16 [3072, 16], replicated, may hold values from -0.109375 to 0.109375
- gate_weight: bfloat16 [32, 3072, 2560], P('seq', None, 'exp'), may hold values from -0.109375 to 0.109375
- up_weight: bfloat16 [32, 3072, 2560], P('seq', None, 'exp'), may hold values from -0.109375 to 0.109375
- down_weight: bfloat16 [32, 2560, 3072], P('seq', 'exp'), may hold values from -0.078125 to 0.078125
- routes: int32 [8192, 2], P('seq'), may hold values from 0 to 15, all different within a row; in each aligned block of 256 rows (0 to 255, 256 to 511, ...) at most 32 rows name the same one
Outputs:
- mixed: bfloat16 [8192, 3072], P(('seq', 'exp'))
The draws below stay inside these ranges and needn't reach their ends.
Inputs may be any that keep to these rules, and one draw needn't show every extreme that they name: `rates`: each head forgets at its own rate. `doc_lengths`: the lengths sum to 8192; the longest is exactly 4096. `routes`: the two experts of a position differ. In each aligned block of 256 rows no expert is named by more than 32 rows, and in some block one expert is named by exactly 32 rows.
All inputs are finite; a program needn't handle non-finite values.
Results may differ from the reference program's by a relative error of at most 0.014.
Values may be sent and summed in bfloat16 or wider, within the bound.
A program may use at most 128 MiB of HBM per device.

```python
import math
import jax
import jax.numpy as jnp
import numpy as np
from jax import lax

D = 3072
H = 32
HD = 128
F = 5120
TOK_S = 256
NDOC = 16
EXPERTS = 16
L = 8192
CAP = 32
SLICE = 640


def draw_rates(key, part):
    uniform_part = jax.random.uniform(key, (H,), jnp.float32)
    log_lower = math.log(1.0 / (16.0 * L))
    log_upper = math.log(1.0 / 30.0)
    return jnp.exp(log_lower + (log_upper - log_lower) * uniform_part)


def block_scale(rng, dims, pieces, smallest, largest):
    gain = 1.0
    for axis_at, shards_of in pieces:
        steps = jax.random.uniform(jax.random.fold_in(jax.random.fold_in(rng, 6), axis_at), (shards_of,), jnp.float32, smallest / len(pieces), largest / len(pieces))
        gain = gain * jnp.repeat(jnp.exp(steps), dims[axis_at] // shards_of).reshape((-1,) + (1,) * (len(dims) - 1 - axis_at))
    return gain


def length_profile(number_of, total, bound, slope):
    weights = [(1 << 20) // math.isqrt(grade ** slope) + 1 for grade in range(2, number_of + 1)]
    rest, counts = total - bound - (number_of - 1), [1] * (number_of - 1)
    while rest > 0:
        free = [i for i in range(number_of - 1) if counts[i] < bound]
        mass, remaining = sum([weights[i] for i in free]), rest
        for i in free:
            extra = min(bound - counts[i], max(1, remaining * weights[i] // mass), rest)
            counts[i] = counts[i] + extra
            rest = rest - extra
    return np.array([bound] + counts)


def ragged(key, amount, total, limit, lean):
    if amount == 2:
        one = jax.random.randint(key, (), max(1, total - limit), min(limit, total - 1) + 1)
        return jnp.stack([one, total - one])
    lengths = jnp.asarray(length_profile(amount, total, limit, lean), jnp.int32)
    pairs = (amount - 1) // 2
    source_of, receiver = lengths[1:1 + 2 * pairs:2], lengths[2:2 + 2 * pairs:2]
    margin = jnp.minimum(source_of - 1, limit - receiver)
    moved = jax.random.randint(jax.random.fold_in(key, 1), (pairs,), 0, 1 << 20) % (margin + 1)
    lengths = lengths.at[1:1 + 2 * pairs:2].set(source_of - moved).at[2:2 + 2 * pairs:2].set(receiver + moved)
    return lengths[jax.random.permutation(jax.random.fold_in(key, 2), amount)]


def deal_out(stream_key, own, number, rows, amount, top, reach, slope):
    order = jax.random.permutation(stream_key, amount)
    packed, ordinary = portions_of(amount, rows * top, reach, slope, True), portions_of(amount, rows * top, reach, slope, False)
    places = jnp.arange(amount)

    def named(tallies, turn):
        used = int((tallies > 0).sum())
        fixed = max(1, used // 4)
        shifted = fixed + (places - fixed + turn * (used - fixed)) % max(1, amount - fixed)
        return jnp.zeros((amount,), jnp.int32).at[order[jnp.where(places < fixed, places, shifted)]].set(jnp.asarray(tallies, jnp.int32))

    tallies = jnp.where(number % 4 == 0, named(packed, number // 4), named(ordinary, number - number // 4 - 1))
    mixed = jax.random.permutation(jax.random.fold_in(own, 3), amount)
    giver, sink = mixed[0:amount // 2 * 2:2], mixed[1:amount // 2 * 2:2]
    slack = jnp.minimum(tallies[giver] - 1, reach - tallies[sink]) // 2
    slack = jnp.where((giver == order[0]) | (sink == order[0]) | (tallies[sink] == 0), 0, jnp.maximum(slack, 0))
    shifted = jax.random.randint(jax.random.fold_in(own, 4), (amount // 2,), 0, 1 << 20) % (slack + 1)
    tallies = tallies.at[giver].add(-shifted).at[sink].add(shifted)
    members = jnp.searchsorted(jnp.cumsum(tallies), jnp.arange(rows * top), side="right").astype(jnp.int32)
    listing = members.reshape(top, rows).T
    listing = listing[jax.random.permutation(jax.random.fold_in(own, 1), rows)]
    turn = jax.random.randint(jax.random.fold_in(own, 2), (rows, 1), 0, top)
    return jnp.take_along_axis(listing, (jnp.arange(top)[None, :] + turn) % top, axis=1)


def portions_of(amount, total, most, skew, full):
    weights = [(1 << 20) // math.isqrt(rank ** skew) + 1 for rank in range(1, amount + 1)]
    largest = most if full else min(most, max(-(-total // amount), total * weights[0] // sum(weights)))
    least = 1 if total - largest >= amount - 1 else 0
    given, spare = [largest] + [least] * (amount - 1), total - largest - least * (amount - 1)
    while spare > 0:
        movable = [i for i in range(1, amount) if given[i] < largest] or [i for i in range(1, amount) if given[i] < most]
        mass, budget = sum([weights[i] for i in movable]), spare
        for i in movable:
            addition = min(most - given[i], max(1, budget * weights[i] // mass), spare)
            given[i] = given[i] + addition
            spare = spare - addition
    return np.array(given)


def bell_draw(own_key, shape, scale, bound, pieces=(), kind=jnp.bfloat16):
    entries = jax.random.normal(own_key, shape, jnp.float32) * scale
    if len(pieces) > 0:
        entries = block_scale(own_key, shape, pieces, -0.22, 0.18) * entries
    return jnp.clip(entries, min=-bound, max=bound).astype(kind)


def setup_inputs(seed: int = 0) -> dict:
    arg_keys = jax.random.split(jax.random.key(seed), 13)
    residual_in = bell_draw(arg_keys[0], (L, D), 1.0, 6.0, ((0, 32),))
    queries = bell_draw(arg_keys[1], (L, H * HD), 1.0, 6.0, ((0, 32), (1, 4)))
    keys = bell_draw(arg_keys[2], (L, H * HD), 1.0, 6.0, ((0, 32), (1, 4)))
    values = bell_draw(arg_keys[3], (L, H * HD), 1.0, 6.0, ((0, 32), (1, 4)))
    rates = draw_rates(jax.random.fold_in(arg_keys[12], 71), 0)
    doc_lengths = ragged(arg_keys[5], NDOC, L, L // 2, 2).astype(jnp.int32)
    out_weight = bell_draw(arg_keys[6], (H * HD, D), (H * HD) ** -0.5, 0.09375, ((0, 4),))
    router = bell_draw(arg_keys[7], (D, EXPERTS), D ** -0.5, 0.109375)
    gate_weight = bell_draw(arg_keys[8], (2 * EXPERTS, D, F // 2), D ** -0.5, 0.109375, ((0, 32), (2, 4)))
    up_weight = bell_draw(arg_keys[9], (2 * EXPERTS, D, F // 2), D ** -0.5, 0.109375, ((0, 32), (2, 4)))
    down_weight = bell_draw(arg_keys[10], (2 * EXPERTS, F // 2, D), F ** -0.5, 0.078125, ((0, 32), (1, 4)))
    routes_keys = jax.random.split(jax.random.fold_in(arg_keys[11], 1), L // TOK_S)
    routes_turns = jax.random.permutation(jax.random.fold_in(arg_keys[11], 3), L // TOK_S)
    routes = jax.vmap(lambda own, number: deal_out(jax.random.fold_in(arg_keys[11], 2), own, number, TOK_S, EXPERTS, 2, CAP, 1))(routes_keys, routes_turns).reshape((L, 2))
    return dict(residual_in=residual_in, queries=queries, keys=keys, values=values, rates=rates, doc_lengths=doc_lengths, out_weight=out_weight, router=router, gate_weight=gate_weight, up_weight=up_weight, down_weight=down_weight, routes=routes)


EPSILON = 1e-06

def rms_rows(rows):
    return rows * lax.rsqrt(lax.optimization_barrier(jnp.mean(rows * rows, axis=-1, keepdims=True)) + EPSILON)

def reference(residual_in, queries, keys, values, rates, doc_lengths, out_weight, router, gate_weight, up_weight, down_weight, routes):
    highest = lax.Precision.HIGHEST
    blocks = L // TOK_S
    position = jnp.arange(L, dtype=jnp.int32)
    doc_starts = (jnp.cumsum(doc_lengths) - doc_lengths).astype(jnp.int32)
    doc_of = (lax.optimization_barrier(jnp.sum((doc_starts[None, :] <= position[:, None]).astype(jnp.int32), axis=1)) - 1).astype(jnp.int32)
    local_index = jnp.arange(TOK_S, dtype=jnp.int32)
    query_heads = queries.reshape(blocks, TOK_S, H, HD)
    key_heads = keys.reshape(blocks, TOK_S, H, HD)
    value_heads = values.reshape(blocks, TOK_S, H, HD)
    doc_blocks = doc_of.reshape(blocks, TOK_S)
    same_last = (doc_blocks == doc_blocks[:, -1:]).astype(jnp.float32)
    distance_end = (TOK_S - local_index).astype(jnp.float32)
    end_weight = jnp.exp(-rates[None, None, :] * distance_end[None, :, None]) * same_last[:, :, None]
    weighted_keys = end_weight[:, :, :, None] * key_heads.astype(jnp.float32)
    block_state = jnp.einsum('ctha,cthb->chab', weighted_keys, value_heads.astype(jnp.float32), precision=highest)
    block_base = jnp.arange(blocks, dtype=jnp.int32) * TOK_S
    first_start = lax.optimization_barrier(jnp.max(jnp.where(doc_starts[None, :] <= block_base[:, None], doc_starts[None, :], 0), axis=1))
    block_end = block_base + TOK_S
    block_ids = jnp.arange(blocks, dtype=jnp.int32)
    usable = (block_ids[None, :] < block_ids[:, None]) & (block_end[None, :] - 1 >= first_start[:, None])
    distance = jnp.maximum(block_base[:, None] - block_end[None, :], 0).astype(jnp.float32)
    weight = jnp.where(usable[:, :, None], jnp.exp(-rates[None, None, :] * distance[:, :, None]), 0.0)
    carried = jnp.einsum('cjh,jhab->chab', weight, block_state, precision=highest)
    carried_rounded = carried.astype(jnp.bfloat16)

    def one_block(inputs):
        query_block, key_block, value_block, carry_block, doc_block = inputs
        query_float = query_block.astype(jnp.float32)
        scores = jnp.einsum('thd,uhd->htu', query_float, key_block.astype(jnp.float32))
        lag_steps = local_index[:, None] - local_index[None, :]
        allowed = (lag_steps >= 0) & (doc_block[:, None] == doc_block[None, :])
        decay_mask = jnp.where(allowed[None], jnp.exp(-rates[:, None, None] * jnp.maximum(lag_steps, 0).astype(jnp.float32)[None]), 0.0)
        probs = (scores * decay_mask).astype(jnp.bfloat16)
        inside_term = jnp.einsum('htu,uhd->thd', probs.astype(jnp.float32), value_block.astype(jnp.float32))
        carried_term = jnp.einsum('thd,hde->the', query_float, carry_block.astype(jnp.float32))
        carry_scale = jnp.exp(-rates[None, :] * local_index.astype(jnp.float32)[:, None]) * (doc_block == doc_block[0]).astype(jnp.float32)[:, None]
        heads_raw = inside_term + carried_term * carry_scale[:, :, None]
        return rms_rows(heads_raw).astype(jnp.bfloat16).reshape(TOK_S, H * HD)
    attn = lax.map(one_block, (query_heads, key_heads, value_heads, carried_rounded, doc_blocks)).reshape(L, H * HD)
    hidden = (residual_in.astype(jnp.float32) + jnp.dot(attn, out_weight, preferred_element_type=jnp.float32)).astype(jnp.bfloat16)
    normed = rms_rows(hidden.astype(jnp.float32)).astype(jnp.bfloat16)
    logits = jnp.dot(normed, router, preferred_element_type=jnp.float32)
    picked_logits = jnp.take_along_axis(logits, routes, axis=1)
    route_weight = jax.nn.sigmoid(picked_logits - picked_logits[:, ::-1])
    pair_expert = routes.reshape(blocks, 2 * TOK_S).astype(jnp.int32)
    expert_ids = jnp.arange(EXPERTS, dtype=jnp.int32)
    onehot = (pair_expert[:, :, None] == expert_ids[None, None, :]).astype(jnp.int32)
    rank_before = (jnp.cumsum(onehot, axis=1) - onehot).astype(jnp.int32)
    slot_index = lax.optimization_barrier(jnp.sum(rank_before * onehot, axis=2)).astype(jnp.int32)
    pair_token = (block_base[:, None] + jnp.arange(2 * TOK_S, dtype=jnp.int32)[None, :] // 2).astype(jnp.int32)
    block_grid = jnp.broadcast_to(block_ids[:, None], pair_expert.shape).astype(jnp.int32)
    row_table = jnp.full((EXPERTS, blocks, CAP), L, jnp.int32).at[pair_expert, block_grid, slot_index].set(pair_token)
    padded_rows = jnp.concatenate([normed, jnp.zeros((1, D), jnp.bfloat16)], axis=0)
    gate_pairs = gate_weight.reshape(EXPERTS, 2, D, F // 2)
    up_pairs = up_weight.reshape(EXPERTS, 2, D, F // 2)
    down_pairs = down_weight.reshape(EXPERTS, 2, F // 2, D)

    def one_expert(inputs):
        table_rows, gate_pair, up_pair, down_pair = inputs
        expert_rows = padded_rows[table_rows.reshape(-1)]
        gate_full = jnp.concatenate([gate_pair[0], gate_pair[1]], axis=1)
        up_full = jnp.concatenate([up_pair[0], up_pair[1]], axis=1)
        down_full = jnp.concatenate([down_pair[0], down_pair[1]], axis=0)
        gate_act = jnp.dot(expert_rows, gate_full, preferred_element_type=jnp.float32)
        up_act = jnp.dot(expert_rows, up_full, preferred_element_type=jnp.float32)
        active = (jax.nn.silu(gate_act) * up_act).astype(jnp.bfloat16)
        running = jnp.zeros((expert_rows.shape[0], D), jnp.float32)
        for slice_number in range(F // SLICE):
            term = jnp.dot(active[:, slice_number * SLICE:(slice_number + 1) * SLICE], down_full[slice_number * SLICE:(slice_number + 1) * SLICE], preferred_element_type=jnp.float32)
            rounded = lax.optimization_barrier(term.astype(jnp.bfloat16))
            running = running + rounded.astype(jnp.float32)
        return running
    expert_out = lax.map(one_expert, (row_table, gate_pairs, up_pairs, down_pairs)).reshape(EXPERTS * blocks * CAP, D)
    flat_index = (pair_expert * (blocks * CAP) + block_grid * CAP + slot_index).reshape(-1).astype(jnp.int32)
    gathered = expert_out[flat_index].reshape(L, 2, D)
    expert_mix = lax.optimization_barrier(jnp.sum(gathered * route_weight[:, :, None], axis=1))
    return (hidden.astype(jnp.float32) + expert_mix).astype(jnp.bfloat16)
```

```python
import functools

import jax
import jax.numpy as jnp
from jax import lax
from jax.experimental import pallas as pl
from jax.experimental.pallas import tpu as pltpu
from jax.sharding import PartitionSpec as P

EPSILON = 1e-06
MESH = pl.DeviceIdType.MESH
F32, BF16, I32 = jnp.float32, jnp.bfloat16, jnp.int32
NSEQ, NZ = 32, 4
TOK, D, HEADS, HS = 256, 3072, 8, 128
OWN = TOK // NZ
HALF = D // 2
SL = 640
VMEM_LIMIT = 63_000_000


def rcopy(src, dst, ssem, rsem, dev):
    return pltpu.make_async_remote_copy(
        src_ref=src, dst_ref=dst, send_sem=ssem, recv_sem=rsem, device_id=dev, device_id_type=MESH
    )


def rows(r, n):
    return pl.ds(pl.multiple_of(r * n, n), n)


def entry_signal(me, z):
    barrier = pltpu.get_barrier_semaphore()

    @pl.loop(1, NSEQ)
    def _(d):
        pl.semaphore_signal(
            barrier, inc=1, device_id=(lax.rem(me + d, NSEQ), z), device_id_type=MESH
        )

    for dz in (1, 3):
        pl.semaphore_signal(
            barrier, inc=1, device_id=(me, lax.rem(z + dz, NZ)), device_id_type=MESH
        )
    return barrier


def entry_wait(barrier):
    pl.semaphore_wait(barrier, NSEQ + 1)


A = slice(0, HALF)
B = slice(HALF, D)


def reduce_scatter_z(me, z, p_ref, relay, acc, got, ssem, rsem):
    right, left, far = lax.rem(z + 1, NZ), lax.rem(z + 3, NZ), lax.rem(z + 2, NZ)
    dr, dl = (me, right), (me, left)
    c1 = rcopy(p_ref.at[rows(far, OWN), A], relay.at[0], ssem.at[0], rsem.at[0], dr)
    c2 = rcopy(p_ref.at[rows(far, OWN), B], relay.at[1], ssem.at[1], rsem.at[1], dl)
    c3 = rcopy(p_ref.at[rows(right, OWN), B], got.at[0, :, B], ssem.at[2], rsem.at[2], dr)
    c4 = rcopy(p_ref.at[rows(left, OWN), A], got.at[1, :, A], ssem.at[3], rsem.at[3], dl)
    for c in (c1, c2, c3, c4):
        c.start()
    c1.wait_recv()
    acc[0] = (p_ref[rows(right, OWN), A].astype(F32) + relay[0].astype(F32)).astype(BF16)
    c5 = rcopy(acc.at[0], got.at[0, :, A], ssem.at[4], rsem.at[4], dr)
    c5.start()
    c2.wait_recv()
    acc[1] = (p_ref[rows(left, OWN), B].astype(F32) + relay[1].astype(F32)).astype(BF16)
    c6 = rcopy(acc.at[1], got.at[1, :, B], ssem.at[5], rsem.at[5], dl)
    c6.start()
    for c in (c3, c4, c5, c6):
        c.wait_recv()
    total = (
        p_ref[rows(z, OWN), :].astype(F32) + got[0].astype(F32) + got[1].astype(F32)
    )
    for c in (c1, c2, c3, c4, c5, c6):
        c.wait_send()
    return total


def all_gather_z(me, z, buf, ssem, rsem):
    right, left = lax.rem(z + 1, NZ), lax.rem(z + 3, NZ)
    dr, dl = (me, right), (me, left)

    def part(owner, cols):
        return buf.at[rows(owner, OWN), cols]

    c1 = rcopy(part(z, A), part(z, A), ssem.at[0], rsem.at[0], dr)
    c2 = rcopy(part(z, B), part(z, B), ssem.at[1], rsem.at[1], dl)
    c3 = rcopy(part(z, B), part(z, B), ssem.at[2], rsem.at[2], dr)
    c4 = rcopy(part(z, A), part(z, A), ssem.at[3], rsem.at[3], dl)
    for c in (c1, c2, c3, c4):
        c.start()
    c1.wait_recv()
    c5 = rcopy(part(left, A), part(left, A), ssem.at[4], rsem.at[4], dr)
    c5.start()
    c2.wait_recv()
    c6 = rcopy(part(right, B), part(right, B), ssem.at[5], rsem.at[5], dl)
    c6.start()
    for c in (c3, c4, c5, c6):
        c.wait_recv()
    for c in (c1, c2, c3, c4, c5, c6):
        c.wait_send()


def attention_kernel(
    rates,
    docs,
    q_ref,
    k_ref,
    v_ref,
    res_hbm,
    wo_hbm,
    normed_out,
    hidden_out,
    wo,
    res,
    st_send,
    st_recv,
    ca_send,
    ca_recv,
    coef,
    inside,
    attn,
    p_ref,
    relay,
    acc,
    got,
    nbuf,
    lsem,
    s1,
    r1,
    s2,
    r2,
    s3,
    r3,
    s4,
    r4,
):
    me, z = lax.axis_index("seq"), lax.axis_index("exp")
    barrier = entry_signal(me, z)
    load_wo = pltpu.make_async_copy(wo_hbm, wo, lsem.at[0])
    load_wo.start()
    load_res = pltpu.make_async_copy(res_hbm.at[rows(z, OWN), :], res, lsem.at[1])
    load_res.start()

    starts = [jnp.int32(0)]
    for i in range(15):
        starts.append(starts[-1] + docs[i])

    def doc_at(pos):
        total = jnp.zeros(pos.shape, I32)
        for s in starts:
            total = total + (pos >= s).astype(I32)
        return total

    base = me * TOK
    t_col = lax.broadcasted_iota(I32, (TOK, 1), 0)
    t_row = lax.broadcasted_iota(I32, (1, TOK), 1)
    doc_col = doc_at(base + t_col)
    doc_row = doc_at(base + t_row)
    doc_first, doc_last = jnp.int32(0), jnp.int32(0)
    for s in starts:
        doc_first = doc_first + (base >= s).astype(I32)
        doc_last = doc_last + (base + TOK - 1 >= s).astype(I32)
    same_last = (doc_col == doc_last).astype(F32)
    same_first = (doc_col == doc_first).astype(F32)
    end_dist = (TOK - t_col).astype(F32)
    local_f = t_col.astype(F32)

    for h in range(HEADS):
        cols = slice(h * HS, (h + 1) * HS)
        w = jnp.exp(-rates[h] * end_dist) * same_last
        kw = (k_ref[:, cols].astype(F32) * w).astype(BF16)
        state = lax.dot_general(
            kw, v_ref[:, cols], (((0,), (0,)), ((), ())), preferred_element_type=F32
        )
        st_send[h * HS : (h + 1) * HS, :] = state.astype(BF16)

    entry_wait(barrier)
    own1 = pltpu.make_async_copy(st_send.at[rows(me, 32), :], st_recv.at[me], lsem.at[2])
    own1.start()

    def send1(d):
        j = lax.rem(me + d, NSEQ)
        return rcopy(
            st_send.at[rows(j, 32), :], st_recv.at[me], s1.at[d], r1.at[me], (j, z)
        )

    @pl.loop(1, NSEQ)
    def _(d):
        send1(d).start()

    lag = lax.broadcasted_iota(I32, (TOK, TOK), 0) - lax.broadcasted_iota(I32, (TOK, TOK), 1)
    allowed = (lag >= 0) & (doc_col == doc_row)
    lag_f = jnp.where(allowed, lag.astype(F32), 3e38)

    def inner(h):
        cols = slice(h * HS, (h + 1) * HS)
        scores = lax.dot_general(
            q_ref[:, cols], k_ref[:, cols], (((1,), (1,)), ((), ())), preferred_element_type=F32
        )
        probs = (scores * jnp.exp(-rates[h] * lag_f)).astype(BF16)
        inside[h] = jnp.dot(probs, v_ref[:, cols], preferred_element_type=F32)

    for h in range(4):
        inner(h)

    own1.wait()

    @pl.loop(1, NSEQ)
    def _(d):
        j = lax.rem(me + d, NSEQ)
        rcopy(st_send.at[rows(j, 32), :], st_recv.at[j], s1.at[d], r1.at[j], (j, z)).wait_recv()

    c_pos = lax.broadcasted_iota(I32, (NSEQ, HS), 0) * TOK
    d_here = doc_at(c_pos)
    u = (d_here == doc_at(c_pos - 1)).astype(F32)
    g = (d_here == doc_at(c_pos - TOK)).astype(F32)
    r_own = rates[me // (NSEQ // HEADS)]
    coef[0] = u
    coef[1] = g * jnp.exp(jnp.full((NSEQ, HS), -float(TOK), F32) * r_own)
    total = jnp.zeros((32, HS), F32)
    ca_send[0] = total.astype(BF16)
    for c in range(1, NSEQ):
        total = coef[1, c : c + 1, :] * total + coef[0, c : c + 1, :] * st_recv[c - 1].astype(F32)
        ca_send[c] = total.astype(BF16)

    own2 = pltpu.make_async_copy(ca_send.at[me], ca_recv.at[me], lsem.at[3])
    own2.start()

    @pl.loop(1, NSEQ)
    def _(d):
        j = lax.rem(me + d, NSEQ)
        rcopy(ca_send.at[j], ca_recv.at[me], s2.at[d], r2.at[me], (j, z)).start()

    for h in range(4, 8):
        inner(h)

    own2.wait()

    @pl.loop(1, NSEQ)
    def _(d):
        j = lax.rem(me + d, NSEQ)
        rcopy(ca_send.at[j], ca_recv.at[j], s2.at[d], r2.at[j], (j, z)).wait_recv()

    for h in range(HEADS):
        cols = slice(h * HS, (h + 1) * HS)
        carried = ca_recv[h * 4 : (h + 1) * 4].reshape(HS, HS)
        term = jnp.dot(q_ref[:, cols], carried, preferred_element_type=F32)
        raw = inside[h] + term * (jnp.exp(-rates[h] * local_f) * same_first)
        scale = lax.rsqrt(jnp.mean(raw * raw, axis=-1, keepdims=True) + EPSILON)
        attn[:, cols] = (raw * scale).astype(BF16)

    load_wo.wait()

    @pl.loop(0, D // 512)
    def _(n):
        cols = rows(n, 512)
        p_ref[:, cols] = jnp.dot(
            attn[...], wo[:, cols], preferred_element_type=F32
        ).astype(BF16)

    share = reduce_scatter_z(me, z, p_ref, relay, acc, got, s3, r3)
    load_res.wait()
    hidden = (res[...].astype(F32) + share).astype(BF16)
    hidden_out[...] = hidden
    hid = hidden.astype(F32)
    scale = lax.rsqrt(jnp.mean(hid * hid, axis=-1, keepdims=True) + EPSILON)
    nbuf[rows(z, OWN), :] = (hid * scale).astype(BF16)
    all_gather_z(me, z, nbuf, s4, r4)
    out = pltpu.make_async_copy(nbuf, normed_out, lsem.at[4])
    out.start()

    @pl.loop(1, NSEQ)
    def _(d):
        j = lax.rem(me + d, NSEQ)
        send1(d).wait_send()
        rcopy(ca_send.at[j], ca_recv.at[me], s2.at[d], r2.at[me], (j, z)).wait_send()

    out.wait()


def expert_kernel(
    routes,
    routes_t,
    router_t,
    hidden,
    normed_hbm,
    gate_hbm,
    up_hbm,
    down_hbm,
    out_ref,
    nbuf,
    wgu,
    wd,
    slots,
    mixw,
    x,
    hbuf,
    abuf,
    y_own,
    y_send,
    y_recv,
    back,
    table,
    p_ref,
    relay,
    acc,
    got,
    lsem,
    s1,
    r1,
    s2,
    r2,
    s3,
    r3,
    s4,
    r4,
    s5,
    r5,
):
    me, z = lax.axis_index("seq"), lax.axis_index("exp")
    chip, core = me // 2, lax.rem(me, 2)
    other = 1 - core
    cx, cy = chip // 4, lax.rem(chip, 4)
    partner = (chip * 2 + other, z)
    barrier = entry_signal(me, z)
    load_n = pltpu.make_async_copy(normed_hbm, nbuf, lsem.at[0])
    load_n.start()
    load_g = pltpu.make_async_copy(gate_hbm.at[0], wgu.at[:, 0:SL], lsem.at[1])
    load_u = pltpu.make_async_copy(up_hbm.at[0], wgu.at[:, SL : 2 * SL], lsem.at[2])
    load_d = pltpu.make_async_copy(down_hbm.at[0], wd, lsem.at[3])
    for c in (load_g, load_u, load_d):
        c.start()

    e_sub = lax.broadcasted_iota(I32, (16, TOK), 0)
    chosen_t = ((routes_t[0:1, :] == e_sub) | (routes_t[1:2, :] == e_sub)).astype(F32).astype(BF16)
    ri = lax.broadcasted_iota(I32, (TOK, TOK), 0)
    ci = lax.broadcasted_iota(I32, (TOK, TOK), 1)
    before_t = (ri < ci).astype(F32).astype(BF16)
    rank_t = jnp.dot(chosen_t, before_t, preferred_element_type=F32).astype(BF16)
    expand_t = (
        lax.broadcasted_iota(I32, (512, 16), 0) // 32 == lax.broadcasted_iota(I32, (512, 16), 1)
    ).astype(F32).astype(BF16)
    rank_big = jnp.dot(expand_t, rank_t, preferred_element_type=F32)
    chosen_big = jnp.dot(expand_t, chosen_t, preferred_element_type=F32)
    rank_want = lax.rem(lax.broadcasted_iota(I32, (512, TOK), 0), 32).astype(F32)
    pick = jnp.where(rank_big == rank_want, chosen_big, 0.0).astype(BF16)
    load_n.wait()

    for n in range(D // 512):
        cols = slice(n * 512, (n + 1) * 512)
        slots[:, cols] = jnp.dot(pick, nbuf[:, cols], preferred_element_type=F32).astype(BF16)

    entry_wait(barrier)

    def out_copy(i):
        stage, dx, k = i // 8, lax.rem(i // 2, 4), lax.rem(i, 2)
        dy = lax.rem(stage - dx + 4, 4)
        e = lax.rem(cx + dx, 4) * 4 + lax.rem(cy + dy, 4)
        return (
            slots.at[rows(e * 2 + k, 16), :],
            x.at[stage, k, rows(dx * 2 + core, 16), :],
            stage,
            dx * 2 + core,
            (e * 2 + k, z),
        )

    src, dst, _, _, _ = out_copy(core)
    own1 = pltpu.make_async_copy(src, dst, lsem.at[4])
    own1.start()
    src, dst, stage, q, dev = out_copy(other)
    first = rcopy(src, dst, s1.at[other], r1.at[0, core], dev)
    first.start()

    def send1(i):
        src, dst, stage, q, dev = out_copy(i)
        return rcopy(src, dst, s1.at[i], r1.at[stage, q], dev)

    @pl.loop(2, 32)
    def _(i):
        send1(i).start()

    lane16 = lax.broadcasted_iota(I32, (TOK, 16), 1)
    one0 = (routes[:, 0:1] == lane16).astype(F32)
    one1 = (routes[:, 1:2] == lane16).astype(F32)
    logits = lax.dot_general(
        nbuf[...], router_t[...], (((1,), (1,)), ((), ())), preferred_element_type=F32
    )
    l0 = jnp.sum(one0 * logits, axis=1, keepdims=True)
    l1 = jnp.sum(one1 * logits, axis=1, keepdims=True)
    weight = one0 * jax.nn.sigmoid(l0 - l1) + one1 * jax.nn.sigmoid(l1 - l0)
    chosen = (one0 + one1).astype(BF16)
    before = (ci < ri).astype(F32).astype(BF16)
    rank = jnp.dot(before, chosen, preferred_element_type=F32).astype(BF16)
    expand = (
        lax.broadcasted_iota(I32, (16, 512), 1) // 32 == lax.broadcasted_iota(I32, (16, 512), 0)
    ).astype(F32).astype(BF16)
    rank_w = jnp.dot(rank, expand, preferred_element_type=F32)
    weight_w = jnp.dot(weight.astype(BF16), expand, preferred_element_type=F32)
    want = lax.rem(lax.broadcasted_iota(I32, (TOK, 512), 1), 32).astype(F32)
    mixw[...] = jnp.where(rank_w == want, weight_w, 0.0).astype(BF16)

    for c in (load_g, load_u, load_d):
        c.wait()

    def ffn(x_view, y_view):
        @pl.loop(0, 5)
        def _(n):
            cols = rows(n, 256)
            hbuf[:, cols] = jnp.dot(x_view[...], wgu[:, cols], preferred_element_type=F32)

        gate, up = hbuf[:, 0:SL], hbuf[:, SL : 2 * SL]
        abuf[...] = (gate * jax.nn.sigmoid(gate) * up).astype(BF16)

        @pl.loop(0, 6)
        def _(n):
            cols = rows(n, 512)
            y_view[:, cols] = jnp.dot(
                abuf[...], wd[:, cols], preferred_element_type=F32
            ).astype(BF16)

    def hand(stage):
        return rcopy(x.at[stage, core], x.at[stage, core], s2.at[stage], r2.at[stage], partner)

    def hand_in(stage):
        return rcopy(x.at[stage, other], x.at[stage, other], s2.at[stage], r2.at[stage], partner)

    def pair(stage):
        return rcopy(y_send.at[stage], y_recv.at[stage], s3.at[stage], r3.at[stage], partner)

    def back_copy(i):
        stage, dx, k = i // 8, lax.rem(i // 2, 4), lax.rem(i, 2)
        dy = lax.rem(stage - dx + 4, 4)
        home = lax.rem(cx - dx + 4, 4) * 4 + lax.rem(cy - dy + 4, 4)
        return (
            back.at[stage, rows(dx * 2 + k, 16), :],
            table.at[rows(me, 16), :],
            (home * 2 + k, z),
        )

    def send_back(i):
        src, dst, dev = back_copy(i)
        return rcopy(src, dst, s4.at[i], r4.at[i - lax.rem(i, 2) + core], dev)

    own4 = pltpu.make_async_copy(
        back.at[0, rows(core, 16), :], table.at[rows(me, 16), :], lsem.at[5]
    )

    def finish(stage):
        pair(stage).wait_recv()
        back[stage] = (y_own[stage].astype(F32) + y_recv[stage].astype(F32)).astype(BF16)

    def arrive(stage, q):
        rcopy(
            x.at[stage, core, rows(q, 16), :],
            x.at[stage, core, rows(q, 16), :],
            s1.at[0],
            r1.at[stage, q],
            partner,
        ).wait_recv()

    def half(stage):
        hand(stage).start()
        ffn(x.at[stage, core], y_own.at[stage])
        hand_in(stage).wait_recv()
        ffn(x.at[stage, other], y_send.at[stage])
        pair(stage).start()

    own1.wait()
    arrive(0, other)

    @pl.loop(2, 8)
    def _(q):
        arrive(0, q)

    half(0)

    @pl.loop(1, 4)
    def _(stage):
        @pl.loop(0, 8)
        def _(q):
            arrive(stage, q)

        half(stage)
        finish(stage - 1)

        @pl.when(stage == 1)
        def _():
            own4.start()
            send_back(other).start()
            @pl.loop(2, 8)
            def _(i):
                send_back(i).start()

        @pl.when(stage > 1)
        def _():
            @pl.loop(0, 8)
            def _(q):
                send_back((stage - 1) * 8 + q).start()

    finish(3)

    @pl.loop(24, 32)
    def _(i):
        send_back(i).start()

    own4.wait()

    def came(i):
        stage, dx, k = i // 8, lax.rem(i // 2, 4), lax.rem(i, 2)
        dy = lax.rem(stage - dx + 4, 4)
        e = lax.rem(cx + dx, 4) * 4 + lax.rem(cy + dy, 4)
        view = table.at[rows(e * 2 + k, 16), :]
        rcopy(view, view, s4.at[0], r4.at[i], partner).wait_recv()

    came(other)

    @pl.loop(2, 32)
    def _(i):
        came(i)

    @pl.loop(0, D // 512)
    def _(n):
        cols = rows(n, 512)
        p_ref[:, cols] = jnp.dot(
            mixw[...], table[:, cols], preferred_element_type=F32
        ).astype(BF16)

    share = reduce_scatter_z(me, z, p_ref, relay, acc, got, s5, r5)
    out_ref[...] = (hidden[...].astype(F32) + share).astype(BF16)

    first.wait_send()

    @pl.loop(2, 32)
    def _(i):
        send1(i).wait_send()

    @pl.loop(0, 4)
    def _(i):
        hand(i).wait_send()
        pair(i).wait_send()

    send_back(other).wait_send()

    @pl.loop(2, 32)
    def _(i):
        send_back(i).wait_send()


VM = pl.BlockSpec(memory_space=pltpu.VMEM)
SM = pl.BlockSpec(memory_space=pltpu.SMEM)
HB = pl.BlockSpec(memory_space=pl.ANY)
DMA = pltpu.SemaphoreType.DMA


def params(cid):
    return pltpu.CompilerParams(
        collective_id=cid, has_side_effects=True, vmem_limit_bytes=VMEM_LIMIT
    )


def body(
    residual_in,
    queries,
    keys,
    values,
    rates,
    doc_lengths,
    out_weight,
    router,
    gate_weight,
    up_weight,
    down_weight,
    routes,
):
    rs_scratch = [
        pltpu.VMEM((TOK, D), BF16),
        pltpu.VMEM((2, OWN, HALF), BF16),
        pltpu.VMEM((2, OWN, HALF), BF16),
        pltpu.VMEM((2, OWN, D), BF16),
    ]
    normed, hidden = pl.pallas_call(
        attention_kernel,
        name="attention",
        out_shape=[
            jax.ShapeDtypeStruct((TOK, D), BF16),
            jax.ShapeDtypeStruct((OWN, D), BF16),
        ],
        in_specs=[SM, SM, VM, VM, VM, HB, HB],
        out_specs=[HB, VM],
        scratch_shapes=[
            pltpu.VMEM((HEADS * HS, D), BF16),
            pltpu.VMEM((OWN, D), BF16),
            pltpu.VMEM((HEADS * HS, HS), BF16),
            pltpu.VMEM((NSEQ, 32, HS), BF16),
            pltpu.VMEM((NSEQ, 32, HS), BF16),
            pltpu.VMEM((NSEQ, 32, HS), BF16),
            pltpu.VMEM((2, NSEQ, HS), F32),
            pltpu.VMEM((HEADS, TOK, HS), F32),
            pltpu.VMEM((TOK, HEADS * HS), BF16),
            *rs_scratch,
            pltpu.VMEM((TOK, D), BF16),
            DMA((5,)),
            DMA((NSEQ,)),
            DMA((NSEQ,)),
            DMA((NSEQ,)),
            DMA((NSEQ,)),
            DMA((6,)),
            DMA((6,)),
            DMA((6,)),
            DMA((6,)),
        ],
        compiler_params=params(0),
    )(rates, doc_lengths, queries, keys, values, residual_in, out_weight)
    return pl.pallas_call(
        expert_kernel,
        name="experts",
        out_shape=jax.ShapeDtypeStruct((OWN, D), BF16),
        in_specs=[VM, VM, VM, VM, HB, HB, HB, HB],
        out_specs=VM,
        scratch_shapes=[
            pltpu.VMEM((TOK, D), BF16),
            pltpu.VMEM((D, 2 * SL), BF16),
            pltpu.VMEM((SL, D), BF16),
            pltpu.VMEM((512, D), BF16),
            pltpu.VMEM((TOK, 512), BF16),
            pltpu.VMEM((4, 2, 128, D), BF16),
            pltpu.VMEM((128, 2 * SL), F32),
            pltpu.VMEM((128, SL), BF16),
            pltpu.VMEM((4, 128, D), BF16),
            pltpu.VMEM((4, 128, D), BF16),
            pltpu.VMEM((4, 128, D), BF16),
            pltpu.VMEM((4, 128, D), BF16),
            pltpu.VMEM((512, D), BF16),
            *rs_scratch,
            DMA((6,)),
            DMA((32,)),
            DMA((4, 8)),
            DMA((4,)),
            DMA((4,)),
            DMA((4,)),
            DMA((4,)),
            DMA((32,)),
            DMA((32,)),
            DMA((6,)),
            DMA((6,)),
        ],
        compiler_params=params(1),
    )(routes, routes.T, router.T, hidden, normed, gate_weight, up_weight, down_weight)


def solution(mesh):
    in_specs = (
        P("seq", None),
        P("seq", "exp"),
        P("seq", "exp"),
        P("seq", "exp"),
        P("exp"),
        P(),
        P("exp", None),
        P(),
        P("seq", None, "exp"),
        P("seq", None, "exp"),
        P("seq", "exp", None),
        P("seq", None),
    )
    out_specs = P(("seq", "exp"), None)
    return jax.shard_map(body, mesh=mesh, in_specs=in_specs, out_specs=out_specs, check_vma=False)
```

```python
import functools

import jax
import jax.numpy as jnp
from jax import lax
from jax.experimental import pallas as pl
from jax.experimental.pallas import tpu as pltpu
from jax.sharding import PartitionSpec as P

EPSILON = 1e-06
MESH = pl.DeviceIdType.MESH
F32, BF16, I32 = jnp.float32, jnp.bfloat16, jnp.int32
NSEQ, NZ = 32, 4
TOK, D, HEADS, HS = 256, 3072, 8, 128
OWN = TOK // NZ
HALF = D // 2
SL = 640
VMEM_LIMIT = 63_000_000


def rcopy(src, dst, ssem, rsem, dev):
    return pltpu.make_async_remote_copy(
        src_ref=src, dst_ref=dst, send_sem=ssem, recv_sem=rsem, device_id=dev, device_id_type=MESH
    )


def rows(r, n):
    return pl.ds(pl.multiple_of(r * n, n), n)


def entry_signal(me, z):
    barrier = pltpu.get_barrier_semaphore()

    @pl.loop(1, NSEQ)
    def _(d):
        pl.semaphore_signal(
            barrier, inc=1, device_id=(lax.rem(me + d, NSEQ), z), device_id_type=MESH
        )

    for dz in (1, 3):
        pl.semaphore_signal(
            barrier, inc=1, device_id=(me, lax.rem(z + dz, NZ)), device_id_type=MESH
        )
    return barrier


def entry_wait(barrier):
    pl.semaphore_wait(barrier, NSEQ + 1)


A = slice(0, HALF)
B = slice(HALF, D)


def reduce_scatter_z(me, z, p_ref, relay, acc, got, ssem, rsem):
    right, left, far = lax.rem(z + 1, NZ), lax.rem(z + 3, NZ), lax.rem(z + 2, NZ)
    dr, dl = (me, right), (me, left)
    c1 = rcopy(p_ref.at[rows(far, OWN), A], relay.at[0], ssem.at[0], rsem.at[0], dr)
    c2 = rcopy(p_ref.at[rows(far, OWN), B], relay.at[1], ssem.at[1], rsem.at[1], dl)
    c3 = rcopy(p_ref.at[rows(right, OWN), B], got.at[0, :, B], ssem.at[2], rsem.at[2], dr)
    c4 = rcopy(p_ref.at[rows(left, OWN), A], got.at[1, :, A], ssem.at[3], rsem.at[3], dl)
    for c in (c1, c2, c3, c4):
        c.start()
    c1.wait_recv()
    acc[0] = (p_ref[rows(right, OWN), A].astype(F32) + relay[0].astype(F32)).astype(BF16)
    c5 = rcopy(acc.at[0], got.at[0, :, A], ssem.at[4], rsem.at[4], dr)
    c5.start()
    c2.wait_recv()
    acc[1] = (p_ref[rows(left, OWN), B].astype(F32) + relay[1].astype(F32)).astype(BF16)
    c6 = rcopy(acc.at[1], got.at[1, :, B], ssem.at[5], rsem.at[5], dl)
    c6.start()
    for c in (c3, c4, c5, c6):
        c.wait_recv()
    total = (
        p_ref[rows(z, OWN), :].astype(F32) + got[0].astype(F32) + got[1].astype(F32)
    )
    for c in (c1, c2, c3, c4, c5, c6):
        c.wait_send()
    return total


def all_gather_z(me, z, buf, ssem, rsem):
    right, left = lax.rem(z + 1, NZ), lax.rem(z + 3, NZ)
    dr, dl = (me, right), (me, left)

    def part(owner, cols):
        return buf.at[rows(owner, OWN), cols]

    c1 = rcopy(part(z, A), part(z, A), ssem.at[0], rsem.at[0], dr)
    c2 = rcopy(part(z, B), part(z, B), ssem.at[1], rsem.at[1], dl)
    c3 = rcopy(part(z, B), part(z, B), ssem.at[2], rsem.at[2], dr)
    c4 = rcopy(part(z, A), part(z, A), ssem.at[3], rsem.at[3], dl)
    for c in (c1, c2, c3, c4):
        c.start()
    c1.wait_recv()
    c5 = rcopy(part(left, A), part(left, A), ssem.at[4], rsem.at[4], dr)
    c5.start()
    c2.wait_recv()
    c6 = rcopy(part(right, B), part(right, B), ssem.at[5], rsem.at[5], dl)
    c6.start()
    for c in (c3, c4, c5, c6):
        c.wait_recv()
    for c in (c1, c2, c3, c4, c5, c6):
        c.wait_send()


def attention_kernel(
    rates,
    docs,
    q_ref,
    k_ref,
    v_ref,
    res_hbm,
    wo_hbm,
    normed_out,
    hidden_out,
    wo,
    res,
    st_send,
    st_recv,
    ca_send,
    ca_recv,
    coef,
    inside,
    attn,
    p_ref,
    relay,
    acc,
    got,
    nbuf,
    lsem,
    s1,
    r1,
    s2,
    r2,
    s3,
    r3,
    s4,
    r4,
):
    me, z = lax.axis_index("seq"), lax.axis_index("exp")
    barrier = entry_signal(me, z)
    load_wo = pltpu.make_async_copy(wo_hbm, wo, lsem.at[0])
    load_wo.start()
    load_res = pltpu.make_async_copy(res_hbm.at[rows(z, OWN), :], res, lsem.at[1])
    load_res.start()

    starts = [jnp.int32(0)]
    for i in range(15):
        starts.append(starts[-1] + docs[i])

    def doc_at(pos):
        total = jnp.zeros(pos.shape, I32)
        for s in starts:
            total = total + (pos >= s).astype(I32)
        return total

    base = me * TOK
    t_col = lax.broadcasted_iota(I32, (TOK, 1), 0)
    t_row = lax.broadcasted_iota(I32, (1, TOK), 1)
    doc_col = doc_at(base + t_col)
    doc_row = doc_at(base + t_row)
    doc_first, doc_last = jnp.int32(0), jnp.int32(0)
    for s in starts:
        doc_first = doc_first + (base >= s).astype(I32)
        doc_last = doc_last + (base + TOK - 1 >= s).astype(I32)
    same_last = (doc_col == doc_last).astype(F32)
    same_first = (doc_col == doc_first).astype(F32)
    end_dist = (TOK - t_col).astype(F32)
    local_f = t_col.astype(F32)

    for h in range(HEADS):
        cols = slice(h * HS, (h + 1) * HS)
        w = jnp.exp(-rates[h] * end_dist) * same_last
        kw = (k_ref[:, cols].astype(F32) * w).astype(BF16)
        state = lax.dot_general(
            kw, v_ref[:, cols], (((0,), (0,)), ((), ())), preferred_element_type=F32
        )
        st_send[h * HS : (h + 1) * HS, :] = state.astype(BF16)

    entry_wait(barrier)
    own1 = pltpu.make_async_copy(st_send.at[rows(me, 32), :], st_recv.at[me], lsem.at[2])
    own1.start()

    def send1(d):
        j = lax.rem(me + d, NSEQ)
        return rcopy(
            st_send.at[rows(j, 32), :], st_recv.at[me], s1.at[d], r1.at[me], (j, z)
        )

    @pl.loop(1, NSEQ)
    def _(d):
        send1(d).start()

    lag = lax.broadcasted_iota(I32, (TOK, TOK), 0) - lax.broadcasted_iota(I32, (TOK, TOK), 1)
    allowed = (lag >= 0) & (doc_col == doc_row)
    lag_f = jnp.where(allowed, lag.astype(F32), 3e38)

    def inner(h):
        cols = slice(h * HS, (h + 1) * HS)
        scores = lax.dot_general(
            q_ref[:, cols], k_ref[:, cols], (((1,), (1,)), ((), ())), preferred_element_type=F32
        )
        probs = (scores * jnp.exp(-rates[h] * lag_f)).astype(BF16)
        inside[h] = jnp.dot(probs, v_ref[:, cols], preferred_element_type=F32)

    for h in range(4):
        inner(h)

    own1.wait()

    @pl.loop(1, NSEQ)
    def _(d):
        j = lax.rem(me + d, NSEQ)
        rcopy(st_send.at[rows(j, 32), :], st_recv.at[j], s1.at[d], r1.at[j], (j, z)).wait_recv()

    c_pos = lax.broadcasted_iota(I32, (NSEQ, HS), 0) * TOK
    d_here = doc_at(c_pos)
    u = (d_here == doc_at(c_pos - 1)).astype(F32)
    g = (d_here == doc_at(c_pos - TOK)).astype(F32)
    r_own = rates[me // (NSEQ // HEADS)]
    coef[0] = u
    coef[1] = g * jnp.exp(jnp.full((NSEQ, HS), -float(TOK), F32) * r_own)
    total = jnp.zeros((32, HS), F32)
    ca_send[0] = total.astype(BF16)
    for c in range(1, NSEQ):
        total = coef[1, c : c + 1, :] * total + coef[0, c : c + 1, :] * st_recv[c - 1].astype(F32)
        ca_send[c] = total.astype(BF16)

    own2 = pltpu.make_async_copy(ca_send.at[me], ca_recv.at[me], lsem.at[3])
    own2.start()

    @pl.loop(1, NSEQ)
    def _(d):
        j = lax.rem(me + d, NSEQ)
        rcopy(ca_send.at[j], ca_recv.at[me], s2.at[d], r2.at[me], (j, z)).start()

    for h in range(4, 8):
        inner(h)

    own2.wait()

    @pl.loop(1, NSEQ)
    def _(d):
        j = lax.rem(me + d, NSEQ)
        rcopy(ca_send.at[j], ca_recv.at[j], s2.at[d], r2.at[j], (j, z)).wait_recv()

    for h in range(HEADS):
        cols = slice(h * HS, (h + 1) * HS)
        carried = ca_recv[h * 4 : (h + 1) * 4].reshape(HS, HS)
        term = jnp.dot(q_ref[:, cols], carried, preferred_element_type=F32)
        raw = inside[h] + term * (jnp.exp(-rates[h] * local_f) * same_first)
        scale = lax.rsqrt(jnp.mean(raw * raw, axis=-1, keepdims=True) + EPSILON)
        attn[:, cols] = (raw * scale).astype(BF16)

    load_wo.wait()

    @pl.loop(0, D // 512)
    def _(n):
        cols = rows(n, 512)
        p_ref[:, cols] = jnp.dot(
            attn[...], wo[:, cols], preferred_element_type=F32
        ).astype(BF16)

    share = reduce_scatter_z(me, z, p_ref, relay, acc, got, s3, r3)
    load_res.wait()
    hidden = (res[...].astype(F32) + share).astype(BF16)
    hidden_out[...] = hidden
    hid = hidden.astype(F32)
    scale = lax.rsqrt(jnp.mean(hid * hid, axis=-1, keepdims=True) + EPSILON)
    nbuf[rows(z, OWN), :] = (hid * scale).astype(BF16)
    all_gather_z(me, z, nbuf, s4, r4)
    out = pltpu.make_async_copy(nbuf, normed_out, lsem.at[4])
    out.start()

    @pl.loop(1, NSEQ)
    def _(d):
        j = lax.rem(me + d, NSEQ)
        send1(d).wait_send()
        rcopy(ca_send.at[j], ca_recv.at[me], s2.at[d], r2.at[me], (j, z)).wait_send()

    out.wait()


def expert_kernel(
    routes,
    routes_t,
    router_t,
    hidden,
    normed_hbm,
    gate_hbm,
    up_hbm,
    down_hbm,
    out_ref,
    nbuf,
    wgu,
    wd,
    slots,
    mixw,
    x,
    hbuf,
    abuf,
    y,
    y_recv,
    back,
    z_recv,
    table,
    p_ref,
    relay,
    acc,
    got,
    lsem,
    s1,
    r1,
    sz,
    rz,
    s2,
    r2,
    s3,
    r3,
    sq,
    rq,
    s4,
    r4,
    s5,
    r5,
):
    me, z = lax.axis_index("seq"), lax.axis_index("exp")
    chip, core = me // 2, lax.rem(me, 2)
    other = 1 - core
    cx, cy = chip // 4, lax.rem(chip, 4)
    partner = (chip * 2 + other, z)
    up_z, down_z = lax.rem(z + 1, NZ), lax.rem(z + 3, NZ)
    parity, level = lax.rem(z, 2), z // 2
    barrier = entry_signal(me, z)
    load_n = pltpu.make_async_copy(normed_hbm, nbuf, lsem.at[0])
    load_n.start()
    load_g = pltpu.make_async_copy(gate_hbm.at[0], wgu.at[:, 0:SL], lsem.at[1])
    load_u = pltpu.make_async_copy(up_hbm.at[0], wgu.at[:, SL : 2 * SL], lsem.at[2])
    load_d = pltpu.make_async_copy(down_hbm.at[0], wd, lsem.at[3])
    for c in (load_g, load_u, load_d):
        c.start()

    def rank_wanted(shape, axis):
        r = lax.broadcasted_iota(I32, shape, axis)
        return (parity * 8 + lax.rem(r // 8, 2) * 16 + lax.rem(r, 8)).astype(F32)

    e_sub = lax.broadcasted_iota(I32, (16, TOK), 0)
    chosen_t = ((routes_t[0:1, :] == e_sub) | (routes_t[1:2, :] == e_sub)).astype(F32).astype(BF16)
    ri = lax.broadcasted_iota(I32, (TOK, TOK), 0)
    ci = lax.broadcasted_iota(I32, (TOK, TOK), 1)
    before_t = (ri < ci).astype(F32).astype(BF16)
    rank_t = jnp.dot(chosen_t, before_t, preferred_element_type=F32).astype(BF16)
    expand_t = (
        lax.broadcasted_iota(I32, (TOK, 16), 0) // 16 == lax.broadcasted_iota(I32, (TOK, 16), 1)
    ).astype(F32).astype(BF16)
    rank_big = jnp.dot(expand_t, rank_t, preferred_element_type=F32)
    chosen_big = jnp.dot(expand_t, chosen_t, preferred_element_type=F32)
    pick = jnp.where(rank_big == rank_wanted((TOK, TOK), 0), chosen_big, 0.0).astype(BF16)
    load_n.wait()

    for n in range(D // 1024):
        cols = slice(n * 1024, (n + 1) * 1024)
        slots[:, cols] = jnp.dot(pick, nbuf[:, cols], preferred_element_type=F32).astype(BF16)

    entry_wait(barrier)

    def away(i, sign):
        stage, dx = i // 4, lax.rem(i, 4)
        dy = lax.rem(stage - dx + 4, 4)
        return lax.rem(cx + sign * dx + 4, 4) * 4 + lax.rem(cy + sign * dy + 4, 4)

    def x_rows(par, unit_par, dx):
        return pl.ds(pl.multiple_of(par * 128 + unit_par * 64 + dx * 16, 16), 16)

    def x_unit(unit, dx):
        r = core * 128 + lax.rem(unit, 2) * 64 + dx * 16 + (unit // 2) * 8
        return pl.ds(pl.multiple_of(r, 8), 8)

    def v_unit(unit, dx):
        r = lax.rem(unit, 2) * 64 + dx * 16 + (unit // 2) * 8
        return pl.ds(pl.multiple_of(r, 8), 8)

    own1 = pltpu.make_async_copy(
        slots.at[rows(chip, 16), :], x.at[0, x_rows(core, parity, 0), :], lsem.at[4]
    )
    own1.start()

    def send1(i):
        stage, dx = i // 4, lax.rem(i, 4)
        e = away(i, 1)
        return rcopy(
            slots.at[rows(e, 16), :],
            x.at[stage, x_rows(core, parity, dx), :],
            s1.at[i],
            r1.at[i],
            (e * 2 + core, z),
        )

    @pl.loop(1, 16)
    def _(i):
        send1(i).start()

    lane16 = lax.broadcasted_iota(I32, (TOK, 16), 1)
    one0 = (routes[:, 0:1] == lane16).astype(F32)
    one1 = (routes[:, 1:2] == lane16).astype(F32)
    logits = lax.dot_general(
        nbuf[...], router_t[...], (((1,), (1,)), ((), ())), preferred_element_type=F32
    )
    l0 = jnp.sum(one0 * logits, axis=1, keepdims=True)
    l1 = jnp.sum(one1 * logits, axis=1, keepdims=True)
    weight = one0 * jax.nn.sigmoid(l0 - l1) + one1 * jax.nn.sigmoid(l1 - l0)
    chosen = (one0 + one1).astype(BF16)
    before = (ci < ri).astype(F32).astype(BF16)
    rank = jnp.dot(before, chosen, preferred_element_type=F32).astype(BF16)
    expand = (
        lax.broadcasted_iota(I32, (16, TOK), 1) // 16 == lax.broadcasted_iota(I32, (16, TOK), 0)
    ).astype(F32).astype(BF16)
    rank_w = jnp.dot(rank, expand, preferred_element_type=F32)
    weight_w = jnp.dot(weight.astype(BF16), expand, preferred_element_type=F32)
    mixw[...] = jnp.where(rank_w == rank_wanted((TOK, TOK), 1), weight_w, 0.0).astype(BF16)

    for c in (load_g, load_u, load_d):
        c.wait()

    def pass_on(stage, dx, side):
        view = x.at[stage, x_unit(z, dx), :]
        to = up_z if side == 0 else down_z
        return rcopy(view, view, sz.at[stage, dx, side], rz.at[stage, dx, side], (me, to))

    def passed(stage, dx, side):
        view = x.at[stage, x_unit(down_z if side == 0 else up_z, dx), :]
        return rcopy(view, view, sz.at[stage, dx, side], rz.at[stage, dx, side], (me, up_z))

    def arrive(stage, first):
        @pl.loop(first, 4)
        def _(dx):
            view = x.at[stage, x_rows(core, parity, dx), :]
            rcopy(view, view, s1.at[0], r1.at[stage * 4 + dx], partner).wait_recv()
            pass_on(stage, dx, 0).start()
            pass_on(stage, dx, 1).start()

    def half(par):
        return pl.ds(pl.multiple_of(par * 128, 128), 128)

    def hand(stage):
        view = x.at[stage, half(core), :]
        return rcopy(view, view, s2.at[stage], r2.at[stage], partner)

    def hand_in(stage):
        view = x.at[stage, half(other), :]
        return rcopy(view, view, s2.at[stage], r2.at[stage], partner)

    def hand_over(stage):
        @pl.loop(0, 4)
        def _(dx):
            passed(stage, dx, 0).wait_recv()
            passed(stage, dx, 1).wait_recv()

        hand(stage).start()

    def pair(stage):
        return rcopy(
            y.at[stage, half(other), :], y_recv.at[stage], s3.at[stage], r3.at[stage], partner
        )

    def z_back(stage, dx, side):
        unit = up_z if side == 0 else down_z
        return rcopy(
            back.at[stage, v_unit(unit, dx), :],
            z_recv.at[stage, side, rows(dx, 8), :],
            sq.at[stage, dx, side],
            rq.at[stage, dx, side],
            (me, unit),
        )

    def pair_sum(stage):
        pair(stage).wait_recv()
        back[stage] = (
            y[stage, half(core), :].astype(F32) + y_recv[stage].astype(F32)
        ).astype(BF16)

        @pl.loop(0, 4)
        def _(dx):
            z_back(stage, dx, 0).start()
            z_back(stage, dx, 1).start()

    def back_rows(dx):
        return pl.ds(pl.multiple_of(parity * 64 + dx * 16, 16), 16)

    def send_back(i):
        stage, dx = i // 4, lax.rem(i, 4)
        return rcopy(
            back.at[stage, back_rows(dx), :],
            table.at[rows(chip, 16), :],
            s4.at[i],
            r4.at[i],
            (away(i, -1) * 2 + core, z),
        )

    own4 = pltpu.make_async_copy(
        back.at[0, back_rows(0), :], table.at[rows(chip, 16), :], lsem.at[5]
    )

    def z_sum(stage):
        @pl.loop(0, 4)
        def _(dx):
            z_back(stage, dx, 0).wait_recv()
            z_back(stage, dx, 1).wait_recv()
            r = v_unit(z, dx)
            back[stage, r, :] = (
                back[stage, r, :].astype(F32)
                + z_recv[stage, 0, rows(dx, 8), :].astype(F32)
                + z_recv[stage, 1, rows(dx, 8), :].astype(F32)
            ).astype(BF16)

        @pl.when(stage == 0)
        def _():
            own4.start()

        @pl.when(stage > 0)
        def _():
            send_back(stage * 4).start()

        @pl.loop(1, 4)
        def _(dx):
            send_back(stage * 4 + dx).start()

    own1.wait()
    pass_on(0, 0, 0).start()
    pass_on(0, 0, 1).start()
    arrive(0, 1)
    hand_over(0)

    @pl.loop(0, 4)
    def _(stage):
        hand_in(stage).wait_recv()

        @pl.when(stage < 3)
        def _():
            arrive(stage + 1, 0)

        hbuf[...] = jnp.dot(x[stage], wgu[...], preferred_element_type=F32)

        @pl.when(stage < 3)
        def _():
            hand_over(stage + 1)

        @pl.when(stage > 0)
        def _():
            pair_sum(stage - 1)

        gate, up = hbuf[:, 0:SL], hbuf[:, SL : 2 * SL]
        abuf[...] = (gate * jax.nn.sigmoid(gate) * up).astype(BF16)

        @pl.loop(0, 3)
        def _(n):
            cols = rows(n, 1024)
            y[stage, :, cols] = jnp.dot(
                abuf[...], wd[:, cols], preferred_element_type=F32
            ).astype(BF16)

        pair(stage).start()

        @pl.when(stage > 0)
        def _():
            z_sum(stage - 1)

    pair_sum(3)
    z_sum(3)
    own4.wait()

    @pl.loop(1, 16)
    def _(i):
        view = table.at[rows(away(i, 1), 16), :]
        rcopy(view, view, s4.at[0], r4.at[i], partner).wait_recv()

    for n in range(D // 1024):
        cols = slice(n * 1024, (n + 1) * 1024)
        p_ref[:, cols] = jnp.dot(
            mixw[...], table[:, cols], preferred_element_type=F32
        ).astype(BF16)

    share = reduce_scatter_z(me, z, p_ref, relay, acc, got, s5, r5)
    out_ref[...] = (hidden[...].astype(F32) + share).astype(BF16)

    @pl.loop(1, 16)
    def _(i):
        send1(i).wait_send()
        send_back(i).wait_send()

    @pl.loop(0, 4)
    def _(i):
        hand(i).wait_send()
        pair(i).wait_send()

        @pl.loop(0, 4)
        def _(dx):
            for side in (0, 1):
                pass_on(i, dx, side).wait_send()
                z_back(i, dx, side).wait_send()


VM = pl.BlockSpec(memory_space=pltpu.VMEM)
SM = pl.BlockSpec(memory_space=pltpu.SMEM)
HB = pl.BlockSpec(memory_space=pl.ANY)
DMA = pltpu.SemaphoreType.DMA


def params(cid):
    return pltpu.CompilerParams(
        collective_id=cid, has_side_effects=True, vmem_limit_bytes=VMEM_LIMIT
    )


def body(
    residual_in,
    queries,
    keys,
    values,
    rates,
    doc_lengths,
    out_weight,
    router,
    gate_weight,
    up_weight,
    down_weight,
    routes,
):
    rs_scratch = [
        pltpu.VMEM((TOK, D), BF16),
        pltpu.VMEM((2, OWN, HALF), BF16),
        pltpu.VMEM((2, OWN, HALF), BF16),
        pltpu.VMEM((2, OWN, D), BF16),
    ]
    normed, hidden = pl.pallas_call(
        attention_kernel,
        name="attention",
        out_shape=[
            jax.ShapeDtypeStruct((TOK, D), BF16),
            jax.ShapeDtypeStruct((OWN, D), BF16),
        ],
        in_specs=[SM, SM, VM, VM, VM, HB, HB],
        out_specs=[HB, VM],
        scratch_shapes=[
            pltpu.VMEM((HEADS * HS, D), BF16),
            pltpu.VMEM((OWN, D), BF16),
            pltpu.VMEM((HEADS * HS, HS), BF16),
            pltpu.VMEM((NSEQ, 32, HS), BF16),
            pltpu.VMEM((NSEQ, 32, HS), BF16),
            pltpu.VMEM((NSEQ, 32, HS), BF16),
            pltpu.VMEM((2, NSEQ, HS), F32),
            pltpu.VMEM((HEADS, TOK, HS), F32),
            pltpu.VMEM((TOK, HEADS * HS), BF16),
            *rs_scratch,
            pltpu.VMEM((TOK, D), BF16),
            DMA((5,)),
            DMA((NSEQ,)),
            DMA((NSEQ,)),
            DMA((NSEQ,)),
            DMA((NSEQ,)),
            DMA((6,)),
            DMA((6,)),
            DMA((6,)),
            DMA((6,)),
        ],
        compiler_params=params(0),
    )(rates, doc_lengths, queries, keys, values, residual_in, out_weight)
    return pl.pallas_call(
        expert_kernel,
        name="experts",
        out_shape=jax.ShapeDtypeStruct((OWN, D), BF16),
        in_specs=[VM, VM, VM, VM, HB, HB, HB, HB],
        out_specs=VM,
        scratch_shapes=[
            pltpu.VMEM((TOK, D), BF16),
            pltpu.VMEM((D, 2 * SL), BF16),
            pltpu.VMEM((SL, D), BF16),
            pltpu.VMEM((TOK, D), BF16),
            pltpu.VMEM((TOK, TOK), BF16),
            pltpu.VMEM((4, TOK, D), BF16),
            pltpu.VMEM((TOK, 2 * SL), F32),
            pltpu.VMEM((TOK, SL), BF16),
            pltpu.VMEM((4, TOK, D), BF16),
            pltpu.VMEM((4, 128, D), BF16),
            pltpu.VMEM((4, 128, D), BF16),
            pltpu.VMEM((4, 2, 32, D), BF16),
            pltpu.VMEM((TOK, D), BF16),
            *rs_scratch,
            DMA((6,)),
            DMA((16,)),
            DMA((16,)),
            DMA((4, 4, 2)),
            DMA((4, 4, 2)),
            DMA((4,)),
            DMA((4,)),
            DMA((4,)),
            DMA((4,)),
            DMA((4, 4, 2)),
            DMA((4, 4, 2)),
            DMA((16,)),
            DMA((16,)),
            DMA((6,)),
            DMA((6,)),
        ],
        compiler_params=params(1),
    )(routes, routes.T, router.T, hidden, normed, gate_weight, up_weight, down_weight)


def solution(mesh):
    in_specs = (
        P("seq", None),
        P("seq", "exp"),
        P("seq", "exp"),
        P("seq", "exp"),
        P("exp"),
        P(),
        P("exp", None),
        P(),
        P("seq", None, "exp"),
        P("seq", None, "exp"),
        P("seq", "exp", None),
        P("seq", None),
    )
    out_specs = P(("seq", "exp"), None)
    return jax.shard_map(body, mesh=mesh, in_specs=in_specs, out_specs=out_specs, check_vma=False)
```

```python
import functools

import jax
import jax.numpy as jnp
from jax import lax
from jax.experimental import pallas as pl
from jax.experimental.pallas import tpu as pltpu
from jax.sharding import PartitionSpec as P

EPSILON = 1e-06
MESH = pl.DeviceIdType.MESH
F32, BF16, I32 = jnp.float32, jnp.bfloat16, jnp.int32
NSEQ, NZ = 32, 4
TOK, D, HEADS, HS = 256, 3072, 8, 128
OWN = TOK // NZ
HALF = D // 2
SL = 640
VMEM_LIMIT = 63_000_000


def rcopy(src, dst, ssem, rsem, dev):
    return pltpu.make_async_remote_copy(
        src_ref=src, dst_ref=dst, send_sem=ssem, recv_sem=rsem, device_id=dev, device_id_type=MESH
    )


def rows(r, n):
    return pl.ds(pl.multiple_of(r * n, n), n)


def entry_signal(me, z):
    barrier = pltpu.get_barrier_semaphore()

    @pl.loop(1, NSEQ)
    def _(d):
        pl.semaphore_signal(
            barrier, inc=1, device_id=(lax.rem(me + d, NSEQ), z), device_id_type=MESH
        )

    for dz in (1, 3):
        pl.semaphore_signal(
            barrier, inc=1, device_id=(me, lax.rem(z + dz, NZ)), device_id_type=MESH
        )
    return barrier


def entry_wait(barrier):
    pl.semaphore_wait(barrier, NSEQ + 1)


A = slice(0, HALF)
B = slice(HALF, D)


def reduce_scatter_z(me, z, p_ref, relay, acc, got, ssem, rsem):
    right, left, far = lax.rem(z + 1, NZ), lax.rem(z + 3, NZ), lax.rem(z + 2, NZ)
    dr, dl = (me, right), (me, left)
    c1 = rcopy(p_ref.at[rows(far, OWN), A], relay.at[0], ssem.at[0], rsem.at[0], dr)
    c2 = rcopy(p_ref.at[rows(far, OWN), B], relay.at[1], ssem.at[1], rsem.at[1], dl)
    c3 = rcopy(p_ref.at[rows(right, OWN), B], got.at[0, :, B], ssem.at[2], rsem.at[2], dr)
    c4 = rcopy(p_ref.at[rows(left, OWN), A], got.at[1, :, A], ssem.at[3], rsem.at[3], dl)
    for c in (c1, c2, c3, c4):
        c.start()
    c1.wait_recv()
    acc[0] = (p_ref[rows(right, OWN), A].astype(F32) + relay[0].astype(F32)).astype(BF16)
    c5 = rcopy(acc.at[0], got.at[0, :, A], ssem.at[4], rsem.at[4], dr)
    c5.start()
    c2.wait_recv()
    acc[1] = (p_ref[rows(left, OWN), B].astype(F32) + relay[1].astype(F32)).astype(BF16)
    c6 = rcopy(acc.at[1], got.at[1, :, B], ssem.at[5], rsem.at[5], dl)
    c6.start()
    for c in (c3, c4, c5, c6):
        c.wait_recv()
    total = (
        p_ref[rows(z, OWN), :].astype(F32) + got[0].astype(F32) + got[1].astype(F32)
    )
    for c in (c1, c2, c3, c4, c5, c6):
        c.wait_send()
    return total


def all_gather_z(me, z, buf, ssem, rsem):
    right, left = lax.rem(z + 1, NZ), lax.rem(z + 3, NZ)
    dr, dl = (me, right), (me, left)

    def part(owner, cols):
        return buf.at[rows(owner, OWN), cols]

    c1 = rcopy(part(z, A), part(z, A), ssem.at[0], rsem.at[0], dr)
    c2 = rcopy(part(z, B), part(z, B), ssem.at[1], rsem.at[1], dl)
    c3 = rcopy(part(z, B), part(z, B), ssem.at[2], rsem.at[2], dr)
    c4 = rcopy(part(z, A), part(z, A), ssem.at[3], rsem.at[3], dl)
    for c in (c1, c2, c3, c4):
        c.start()
    c1.wait_recv()
    c5 = rcopy(part(left, A), part(left, A), ssem.at[4], rsem.at[4], dr)
    c5.start()
    c2.wait_recv()
    c6 = rcopy(part(right, B), part(right, B), ssem.at[5], rsem.at[5], dl)
    c6.start()
    for c in (c3, c4, c5, c6):
        c.wait_recv()
    for c in (c1, c2, c3, c4, c5, c6):
        c.wait_send()


def layer_kernel(
    rates,
    docs,
    q_ref,
    k_ref,
    v_ref,
    routes_t,
    router_t,
    res_hbm,
    wo_hbm,
    gate_hbm,
    up_hbm,
    down_hbm,
    out_ref,
    *scratch,
):
    (
        (wo, res, st_send, st_recv, ca_send, ca_recv, coef, inside, attn, kept),
        (p_ref, relay, acc, got, relay2, acc2, got2),
        (nbuf, wgu, wd, pick, ones, hit, slots, mixw, x, hbuf, abuf, y, y_recv, back, z_recv, table),
        (alsem, as1, ar1, as2, ar2, as3, ar3, as4, ar4),
        (lsem, s1, r1, sz, rz, s2, r2, s3, r3, sq, rq, s4, r4, s5, r5),
    ) = jax.tree.unflatten(SCRATCH_TREE, scratch)
    me, z = lax.axis_index("seq"), lax.axis_index("exp")
    chip, core = me // 2, lax.rem(me, 2)
    other = 1 - core
    cx, cy = chip // 4, lax.rem(chip, 4)
    partner = (chip * 2 + other, z)
    up_z, down_z = lax.rem(z + 1, NZ), lax.rem(z + 3, NZ)
    parity, level = lax.rem(z, 2), z // 2
    barrier = entry_signal(me, z)
    load_wo = pltpu.make_async_copy(wo_hbm, wo, alsem.at[0])
    load_wo.start()
    load_res = pltpu.make_async_copy(res_hbm.at[rows(z, OWN), :], res, alsem.at[1])
    load_res.start()
    load_g = pltpu.make_async_copy(gate_hbm.at[0], wgu.at[:, 0:SL], lsem.at[1])
    load_u = pltpu.make_async_copy(up_hbm.at[0], wgu.at[:, SL : 2 * SL], lsem.at[2])
    load_d = pltpu.make_async_copy(down_hbm.at[0], wd, lsem.at[3])
    for c in (load_g, load_u, load_d):
        c.start()

    starts = [jnp.int32(0)]
    for i in range(15):
        starts.append(starts[-1] + docs[i])

    def doc_at(pos):
        total = jnp.zeros(pos.shape, I32)
        for s in starts:
            total = total + (pos >= s).astype(I32)
        return total

    base = me * TOK
    t_col = lax.broadcasted_iota(I32, (TOK, 1), 0)
    t_row = lax.broadcasted_iota(I32, (1, TOK), 1)
    doc_col = doc_at(base + t_col)
    doc_row = doc_at(base + t_row)
    doc_first, doc_last = jnp.int32(0), jnp.int32(0)
    for s in starts:
        doc_first = doc_first + (base >= s).astype(I32)
        doc_last = doc_last + (base + TOK - 1 >= s).astype(I32)
    same_last = (doc_col == doc_last).astype(F32)
    same_first = (doc_col == doc_first).astype(F32)
    end_dist = (TOK - t_col).astype(F32)
    local_f = t_col.astype(F32)

    for h in range(HEADS):
        cols = slice(h * HS, (h + 1) * HS)
        w = jnp.exp(-rates[h] * end_dist) * same_last
        kw = (k_ref[:, cols].astype(F32) * w).astype(BF16)
        state = lax.dot_general(
            kw, v_ref[:, cols], (((0,), (0,)), ((), ())), preferred_element_type=F32
        )
        st_send[h * HS : (h + 1) * HS, :] = state.astype(BF16)

    entry_wait(barrier)
    own_st = pltpu.make_async_copy(st_send.at[rows(me, 32), :], st_recv.at[me], alsem.at[2])
    own_st.start()

    def send_state(d):
        j = lax.rem(me + d, NSEQ)
        return rcopy(
            st_send.at[rows(j, 32), :], st_recv.at[me], as1.at[d], ar1.at[me], (j, z)
        )

    @pl.loop(1, NSEQ)
    def _(d):
        send_state(d).start()

    lag = lax.broadcasted_iota(I32, (TOK, TOK), 0) - lax.broadcasted_iota(I32, (TOK, TOK), 1)
    allowed = (lag >= 0) & (doc_col == doc_row)
    lag_f = jnp.where(allowed, lag.astype(F32), 3e38)

    def inner(h):
        cols = slice(h * HS, (h + 1) * HS)
        scores = lax.dot_general(
            q_ref[:, cols], k_ref[:, cols], (((1,), (1,)), ((), ())), preferred_element_type=F32
        )
        probs = (scores * jnp.exp(-rates[h] * lag_f)).astype(BF16)
        inside[h] = jnp.dot(probs, v_ref[:, cols], preferred_element_type=F32)

    for h in range(6):
        inner(h)

    own_st.wait()

    @pl.loop(1, NSEQ)
    def _(d):
        j = lax.rem(me + d, NSEQ)
        rcopy(st_send.at[rows(j, 32), :], st_recv.at[j], as1.at[d], ar1.at[j], (j, z)).wait_recv()

    c_pos = lax.broadcasted_iota(I32, (NSEQ, HS), 0) * TOK
    d_here = doc_at(c_pos)
    u = (d_here == doc_at(c_pos - 1)).astype(F32)
    g = (d_here == doc_at(c_pos - TOK)).astype(F32)
    r_own = rates[me // (NSEQ // HEADS)]
    coef[0] = u
    coef[1] = g * jnp.exp(jnp.full((NSEQ, HS), -float(TOK), F32) * r_own)
    total = jnp.zeros((32, HS), F32)
    ca_send[0] = total.astype(BF16)
    for c in range(1, NSEQ):
        total = coef[1, c : c + 1, :] * total + coef[0, c : c + 1, :] * st_recv[c - 1].astype(F32)
        ca_send[c] = total.astype(BF16)

    own_ca = pltpu.make_async_copy(ca_send.at[me], ca_recv.at[me], alsem.at[3])
    own_ca.start()

    @pl.loop(1, NSEQ)
    def _(d):
        j = lax.rem(me + d, NSEQ)
        rcopy(ca_send.at[j], ca_recv.at[me], as2.at[d], ar2.at[me], (j, z)).start()

    for h in range(6, 8):
        inner(h)

    def rank_wanted(shape, axis):
        r = lax.broadcasted_iota(I32, shape, axis)
        return (parity * 8 + lax.rem(r // 8, 2) * 16 + lax.rem(r, 8)).astype(F32)

    def onehot(flag):
        return flag.astype(F32).astype(BF16)

    def flip(a):
        return lax.dot_general(a, eye, (((0,), (0,)), ((), ())), preferred_element_type=F32)

    e_sub = lax.broadcasted_iota(I32, (16, TOK), 0)
    one0_t = onehot(routes_t[0:1, :] == e_sub)
    one1_t = onehot(routes_t[1:2, :] == e_sub)
    chosen_t = one0_t + one1_t
    before_t = onehot(
        lax.broadcasted_iota(I32, (TOK, TOK), 0) < lax.broadcasted_iota(I32, (TOK, TOK), 1)
    )
    rank_t = jnp.dot(chosen_t, before_t, preferred_element_type=F32).astype(BF16)
    expand_t = onehot(
        lax.broadcasted_iota(I32, (TOK, 16), 0) // 16 == lax.broadcasted_iota(I32, (TOK, 16), 1)
    )
    rank_big = jnp.dot(expand_t, rank_t, preferred_element_type=F32)
    chosen_big = jnp.dot(expand_t, chosen_t, preferred_element_type=F32)
    pick[...] = jnp.where(rank_big == rank_wanted((TOK, 1), 0), chosen_big, 0.0).astype(BF16)
    eye = onehot(
        lax.broadcasted_iota(I32, (16, 16), 0) == lax.broadcasted_iota(I32, (16, 16), 1)
    )
    ones[0] = flip(one0_t)
    ones[1] = flip(one1_t)
    expand = onehot(
        lax.broadcasted_iota(I32, (16, TOK), 1) // 16 == lax.broadcasted_iota(I32, (16, TOK), 0)
    )
    rank_w = jnp.dot(flip(rank_t).astype(BF16), expand, preferred_element_type=F32)
    hit[...] = (rank_w == rank_wanted((1, TOK), 1)).astype(F32)

    own_ca.wait()

    @pl.loop(1, NSEQ)
    def _(d):
        j = lax.rem(me + d, NSEQ)
        rcopy(ca_send.at[j], ca_recv.at[j], as2.at[d], ar2.at[j], (j, z)).wait_recv()

    for h in range(HEADS):
        cols = slice(h * HS, (h + 1) * HS)
        carried = ca_recv[h * 4 : (h + 1) * 4].reshape(HS, HS)
        term = jnp.dot(q_ref[:, cols], carried, preferred_element_type=F32)
        raw = inside[h] + term * (jnp.exp(-rates[h] * local_f) * same_first)
        scale = lax.rsqrt(jnp.mean(raw * raw, axis=-1, keepdims=True) + EPSILON)
        attn[:, cols] = (raw * scale).astype(BF16)

    load_wo.wait()

    @pl.loop(0, D // 512)
    def _(n):
        cols = rows(n, 512)
        p_ref[:, cols] = jnp.dot(
            attn[...], wo[:, cols], preferred_element_type=F32
        ).astype(BF16)

    share = reduce_scatter_z(me, z, p_ref, relay, acc, got, as3, ar3)
    load_res.wait()
    hidden = (res[...].astype(F32) + share).astype(BF16)
    kept[...] = hidden
    hid = hidden.astype(F32)
    scale = lax.rsqrt(jnp.mean(hid * hid, axis=-1, keepdims=True) + EPSILON)
    nbuf[rows(z, OWN), :] = (hid * scale).astype(BF16)
    all_gather_z(me, z, nbuf, as4, ar4)

    for n in range(D // 1024):
        cols = slice(n * 1024, (n + 1) * 1024)
        slots[:, cols] = jnp.dot(pick[...], nbuf[:, cols], preferred_element_type=F32).astype(BF16)

    def away(i, sign):
        stage, dx = i // 4, lax.rem(i, 4)
        dy = lax.rem(stage - dx + 4, 4)
        return lax.rem(cx + sign * dx + 4, 4) * 4 + lax.rem(cy + sign * dy + 4, 4)

    def x_rows(par, unit_par, dx):
        return pl.ds(pl.multiple_of(par * 128 + unit_par * 64 + dx * 16, 16), 16)

    def x_unit(unit, dx):
        r = core * 128 + lax.rem(unit, 2) * 64 + dx * 16 + (unit // 2) * 8
        return pl.ds(pl.multiple_of(r, 8), 8)

    def v_unit(unit, dx):
        r = lax.rem(unit, 2) * 64 + dx * 16 + (unit // 2) * 8
        return pl.ds(pl.multiple_of(r, 8), 8)

    own1 = pltpu.make_async_copy(
        slots.at[rows(chip, 16), :], x.at[0, x_rows(core, parity, 0), :], lsem.at[4]
    )
    own1.start()

    def send1(i):
        stage, dx = i // 4, lax.rem(i, 4)
        e = away(i, 1)
        return rcopy(
            slots.at[rows(e, 16), :],
            x.at[stage, x_rows(core, parity, dx), :],
            s1.at[i],
            r1.at[i],
            (e * 2 + core, z),
        )

    @pl.loop(1, 16)
    def _(i):
        send1(i).start()

    logits = lax.dot_general(
        nbuf[...], router_t[...], (((1,), (1,)), ((), ())), preferred_element_type=F32
    )
    one0, one1 = ones[0], ones[1]
    l0 = jnp.sum(one0 * logits, axis=1, keepdims=True)
    l1 = jnp.sum(one1 * logits, axis=1, keepdims=True)
    weight = one0 * jax.nn.sigmoid(l0 - l1) + one1 * jax.nn.sigmoid(l1 - l0)
    expand = onehot(
        lax.broadcasted_iota(I32, (16, TOK), 1) // 16 == lax.broadcasted_iota(I32, (16, TOK), 0)
    )
    weight_w = jnp.dot(weight.astype(BF16), expand, preferred_element_type=F32)
    mixw[...] = (weight_w * hit[...]).astype(BF16)

    for c in (load_g, load_u, load_d):
        c.wait()

    def pass_on(stage, dx, side):
        view = x.at[stage, x_unit(z, dx), :]
        to = up_z if side == 0 else down_z
        return rcopy(view, view, sz.at[stage, dx, side], rz.at[stage, dx, side], (me, to))

    def passed(stage, dx, side):
        view = x.at[stage, x_unit(down_z if side == 0 else up_z, dx), :]
        return rcopy(view, view, sz.at[stage, dx, side], rz.at[stage, dx, side], (me, up_z))

    def arrive(stage, first):
        @pl.loop(first, 4)
        def _(dx):
            view = x.at[stage, x_rows(core, parity, dx), :]
            rcopy(view, view, s1.at[0], r1.at[stage * 4 + dx], partner).wait_recv()
            pass_on(stage, dx, 0).start()
            pass_on(stage, dx, 1).start()

    def half(par):
        return pl.ds(pl.multiple_of(par * 128, 128), 128)

    def hand(stage):
        view = x.at[stage, half(core), :]
        return rcopy(view, view, s2.at[stage], r2.at[stage], partner)

    def hand_in(stage):
        view = x.at[stage, half(other), :]
        return rcopy(view, view, s2.at[stage], r2.at[stage], partner)

    def hand_over(stage):
        @pl.loop(0, 4)
        def _(dx):
            passed(stage, dx, 0).wait_recv()
            passed(stage, dx, 1).wait_recv()

        hand(stage).start()

    def pair(stage):
        return rcopy(
            y.at[stage, half(other), :], y_recv.at[stage], s3.at[stage], r3.at[stage], partner
        )

    def z_back(stage, dx, side):
        unit = up_z if side == 0 else down_z
        return rcopy(
            back.at[stage, v_unit(unit, dx), :],
            z_recv.at[stage, side, rows(dx, 8), :],
            sq.at[stage, dx, side],
            rq.at[stage, dx, side],
            (me, unit),
        )

    def pair_sum(stage):
        pair(stage).wait_recv()
        back[stage] = (
            y[stage, half(core), :].astype(F32) + y_recv[stage].astype(F32)
        ).astype(BF16)

        @pl.loop(0, 4)
        def _(dx):
            z_back(stage, dx, 0).start()
            z_back(stage, dx, 1).start()

    def back_rows(dx):
        return pl.ds(pl.multiple_of(parity * 64 + dx * 16, 16), 16)

    def send_back(i):
        stage, dx = i // 4, lax.rem(i, 4)
        return rcopy(
            back.at[stage, back_rows(dx), :],
            table.at[rows(chip, 16), :],
            s4.at[i],
            r4.at[i],
            (away(i, -1) * 2 + core, z),
        )

    own4 = pltpu.make_async_copy(
        back.at[0, back_rows(0), :], table.at[rows(chip, 16), :], lsem.at[5]
    )

    def z_sum(stage):
        @pl.loop(0, 4)
        def _(dx):
            z_back(stage, dx, 0).wait_recv()
            z_back(stage, dx, 1).wait_recv()
            r = v_unit(z, dx)
            back[stage, r, :] = (
                back[stage, r, :].astype(F32)
                + z_recv[stage, 0, rows(dx, 8), :].astype(F32)
                + z_recv[stage, 1, rows(dx, 8), :].astype(F32)
            ).astype(BF16)

        @pl.when(stage == 0)
        def _():
            own4.start()

        @pl.when(stage > 0)
        def _():
            send_back(stage * 4).start()

        @pl.loop(1, 4)
        def _(dx):
            send_back(stage * 4 + dx).start()

    own1.wait()
    pass_on(0, 0, 0).start()
    pass_on(0, 0, 1).start()
    arrive(0, 1)
    hand_over(0)

    @pl.loop(0, 4)
    def _(stage):
        hand_in(stage).wait_recv()

        @pl.when(stage < 3)
        def _():
            arrive(stage + 1, 0)

        hbuf[...] = jnp.dot(x[stage], wgu[...], preferred_element_type=F32)

        @pl.when(stage < 3)
        def _():
            hand_over(stage + 1)

        @pl.when(stage > 0)
        def _():
            pair_sum(stage - 1)

        gate, up = hbuf[:, 0:SL], hbuf[:, SL : 2 * SL]
        abuf[...] = (gate * jax.nn.sigmoid(gate) * up).astype(BF16)

        @pl.loop(0, 3)
        def _(n):
            cols = rows(n, 1024)
            y[stage, :, cols] = jnp.dot(
                abuf[...], wd[:, cols], preferred_element_type=F32
            ).astype(BF16)

        pair(stage).start()

        @pl.when(stage > 0)
        def _():
            z_sum(stage - 1)

    pair_sum(3)
    z_sum(3)
    own4.wait()

    @pl.loop(1, 16)
    def _(i):
        view = table.at[rows(away(i, 1), 16), :]
        rcopy(view, view, s4.at[0], r4.at[i], partner).wait_recv()

    for n in range(D // 1024):
        cols = slice(n * 1024, (n + 1) * 1024)
        p_ref[:, cols] = jnp.dot(
            mixw[...], table[:, cols], preferred_element_type=F32
        ).astype(BF16)

    share = reduce_scatter_z(me, z, p_ref, relay2, acc2, got2, s5, r5)
    out_ref[...] = (kept[...].astype(F32) + share).astype(BF16)

    @pl.loop(1, 16)
    def _(i):
        send1(i).wait_send()
        send_back(i).wait_send()

    @pl.loop(0, 4)
    def _(i):
        hand(i).wait_send()
        pair(i).wait_send()

        @pl.loop(0, 4)
        def _(dx):
            for side in (0, 1):
                pass_on(i, dx, side).wait_send()
                z_back(i, dx, side).wait_send()

    @pl.loop(1, NSEQ)
    def _(d):
        j = lax.rem(me + d, NSEQ)
        send_state(d).wait_send()
        rcopy(ca_send.at[j], ca_recv.at[me], as2.at[d], ar2.at[me], (j, z)).wait_send()


VM = pl.BlockSpec(memory_space=pltpu.VMEM)
SM = pl.BlockSpec(memory_space=pltpu.SMEM)
HB = pl.BlockSpec(memory_space=pl.ANY)
DMA = pltpu.SemaphoreType.DMA
V = pltpu.VMEM

SCRATCH = (
    (
        V((HEADS * HS, D), BF16),
        V((OWN, D), BF16),
        V((HEADS * HS, HS), BF16),
        V((NSEQ, 32, HS), BF16),
        V((NSEQ, 32, HS), BF16),
        V((NSEQ, 32, HS), BF16),
        V((2, NSEQ, HS), F32),
        V((HEADS, TOK, HS), F32),
        V((TOK, HEADS * HS), BF16),
        V((OWN, D), BF16),
    ),
    (
        V((TOK, D), BF16),
        V((2, OWN, HALF), BF16),
        V((2, OWN, HALF), BF16),
        V((2, OWN, D), BF16),
        V((2, OWN, HALF), BF16),
        V((2, OWN, HALF), BF16),
        V((2, OWN, D), BF16),
    ),
    (
        V((TOK, D), BF16),
        V((D, 2 * SL), BF16),
        V((SL, D), BF16),
        V((TOK, TOK), BF16),
        V((2, TOK, 16), F32),
        V((TOK, TOK), F32),
        V((TOK, D), BF16),
        V((TOK, TOK), BF16),
        V((4, TOK, D), BF16),
        V((TOK, 2 * SL), F32),
        V((TOK, SL), BF16),
        V((4, TOK, D), BF16),
        V((4, 128, D), BF16),
        V((4, 128, D), BF16),
        V((4, 2, 32, D), BF16),
        V((TOK, D), BF16),
    ),
    tuple(DMA((n,)) for n in (5, NSEQ, NSEQ, NSEQ, NSEQ, 6, 6, 6, 6)),
    (
        DMA((6,)),
        DMA((16,)),
        DMA((16,)),
        DMA((4, 4, 2)),
        DMA((4, 4, 2)),
        DMA((4,)),
        DMA((4,)),
        DMA((4,)),
        DMA((4,)),
        DMA((4, 4, 2)),
        DMA((4, 4, 2)),
        DMA((16,)),
        DMA((16,)),
        DMA((6,)),
        DMA((6,)),
    ),
)
SCRATCH_LIST, SCRATCH_TREE = jax.tree.flatten(SCRATCH)


def body(
    residual_in,
    queries,
    keys,
    values,
    rates,
    doc_lengths,
    out_weight,
    router,
    gate_weight,
    up_weight,
    down_weight,
    routes,
):
    return pl.pallas_call(
        layer_kernel,
        name="layer",
        out_shape=jax.ShapeDtypeStruct((OWN, D), BF16),
        in_specs=[SM, SM, VM, VM, VM, VM, VM, HB, HB, HB, HB, HB],
        out_specs=VM,
        scratch_shapes=SCRATCH_LIST,
        compiler_params=pltpu.CompilerParams(
            collective_id=0, has_side_effects=True, vmem_limit_bytes=VMEM_LIMIT
        ),
    )(
        rates,
        doc_lengths,
        queries,
        keys,
        values,
        routes.T,
        router.T,
        residual_in,
        out_weight,
        gate_weight,
        up_weight,
        down_weight,
    )


def solution(mesh):
    in_specs = (
        P("seq", None),
        P("seq", "exp"),
        P("seq", "exp"),
        P("seq", "exp"),
        P("exp"),
        P(),
        P("exp", None),
        P(),
        P("seq", None, "exp"),
        P("seq", None, "exp"),
        P("seq", "exp", None),
        P("seq", None),
    )
    out_specs = P(("seq", "exp"), None)
    return jax.shard_map(body, mesh=mesh, in_specs=in_specs, out_specs=out_specs, check_vma=False)
```

```python
import functools

import jax
import jax.numpy as jnp
from jax import lax
from jax.experimental import pallas as pl
from jax.experimental.pallas import tpu as pltpu
from jax.sharding import PartitionSpec as P

EPSILON = 1e-06
MESH = pl.DeviceIdType.MESH
F32, BF16, I32 = jnp.float32, jnp.bfloat16, jnp.int32
NSEQ, NZ = 32, 4
TOK, D, HEADS, HS = 256, 3072, 8, 128
OWN = TOK // NZ
HALF = D // 2
SL = 640
VMEM_LIMIT = 63_000_000
STAGES = ((0, 4), (4, 4), (8, 4), (12, 4))


def rcopy(src, dst, ssem, rsem, dev):
    return pltpu.make_async_remote_copy(
        src_ref=src, dst_ref=dst, send_sem=ssem, recv_sem=rsem, device_id=dev, device_id_type=MESH
    )


def rows(r, n):
    return pl.ds(pl.multiple_of(r * n, n), n)


def entry_signal(me, z):
    barrier = pltpu.get_barrier_semaphore()

    @pl.loop(1, NSEQ)
    def _(d):
        pl.semaphore_signal(
            barrier, inc=1, device_id=(lax.rem(me + d, NSEQ), z), device_id_type=MESH
        )

    for dz in (1, 3):
        pl.semaphore_signal(
            barrier, inc=1, device_id=(me, lax.rem(z + dz, NZ)), device_id_type=MESH
        )
    return barrier


def entry_wait(barrier):
    pl.semaphore_wait(barrier, NSEQ + 1)


A = slice(0, HALF)
B = slice(HALF, D)
HALVES = (A, B)


def reduce_scatter_z(me, z, make, p_ref, relay, acc, got, ssem, rsem):
    right, left, far = lax.rem(z + 1, NZ), lax.rem(z + 3, NZ), lax.rem(z + 2, NZ)
    dr, dl = (me, right), (me, left)
    c1 = rcopy(p_ref.at[rows(far, OWN), A], relay.at[0], ssem.at[0], rsem.at[0], dr)
    c2 = rcopy(p_ref.at[rows(far, OWN), B], relay.at[1], ssem.at[1], rsem.at[1], dl)
    c3 = rcopy(p_ref.at[rows(right, OWN), B], got.at[0, :, B], ssem.at[2], rsem.at[2], dr)
    c4 = rcopy(p_ref.at[rows(left, OWN), A], got.at[1, :, A], ssem.at[3], rsem.at[3], dl)
    make(0)
    c1.start()
    c4.start()
    make(1)
    c2.start()
    c3.start()
    c1.wait_recv()
    acc[0] = (p_ref[rows(right, OWN), A].astype(F32) + relay[0].astype(F32)).astype(BF16)
    c5 = rcopy(acc.at[0], got.at[0, :, A], ssem.at[4], rsem.at[4], dr)
    c5.start()
    c2.wait_recv()
    acc[1] = (p_ref[rows(left, OWN), B].astype(F32) + relay[1].astype(F32)).astype(BF16)
    c6 = rcopy(acc.at[1], got.at[1, :, B], ssem.at[5], rsem.at[5], dl)
    c6.start()
    for c in (c3, c4, c5, c6):
        c.wait_recv()
    total = (
        p_ref[rows(z, OWN), :].astype(F32) + got[0].astype(F32) + got[1].astype(F32)
    )
    for c in (c1, c2, c3, c4, c5, c6):
        c.wait_send()
    return total


def all_gather_z(me, z, buf, ssem, rsem):
    right, left = lax.rem(z + 1, NZ), lax.rem(z + 3, NZ)
    dr, dl = (me, right), (me, left)

    def part(owner, cols):
        return buf.at[rows(owner, OWN), cols]

    c1 = rcopy(part(z, A), part(z, A), ssem.at[0], rsem.at[0], dr)
    c2 = rcopy(part(z, B), part(z, B), ssem.at[1], rsem.at[1], dl)
    c3 = rcopy(part(z, B), part(z, B), ssem.at[2], rsem.at[2], dr)
    c4 = rcopy(part(z, A), part(z, A), ssem.at[3], rsem.at[3], dl)
    for c in (c1, c2, c3, c4):
        c.start()
    c1.wait_recv()
    c5 = rcopy(part(left, A), part(left, A), ssem.at[4], rsem.at[4], dr)
    c5.start()
    c2.wait_recv()
    c6 = rcopy(part(right, B), part(right, B), ssem.at[5], rsem.at[5], dl)
    c6.start()
    for c in (c3, c4, c5, c6):
        c.wait_recv()
    for c in (c1, c2, c3, c4, c5, c6):
        c.wait_send()


def layer_kernel(
    rates,
    docs,
    q_ref,
    k_ref,
    v_ref,
    routes_t,
    router_t,
    res_hbm,
    wo_hbm,
    gate_hbm,
    up_hbm,
    down_hbm,
    out_ref,
    *scratch,
):
    (
        (wo, res, st_send, st_recv, ca_send, ca_recv, coef, inside, attn, kept),
        (p_ref, relay, acc, got, relay2, acc2, got2),
        (nbuf, wgu, wd, pick, ones, hit, slots, mixw, x, hbuf, abuf, y, y_recv, back, z_recv, table),
        (alsem, as1, ar1, as2, ar2, as3, ar3, as4, ar4),
        (lsem, s1, r1, sz, rz, s2, r2, s3, r3, sq, rq, s4, r4, s5, r5),
    ) = jax.tree.unflatten(SCRATCH_TREE, scratch)
    me, z = lax.axis_index("seq"), lax.axis_index("exp")
    chip, core = me // 2, lax.rem(me, 2)
    other = 1 - core
    cx, cy = chip // 4, lax.rem(chip, 4)
    partner = (chip * 2 + other, z)
    up_z, down_z = lax.rem(z + 1, NZ), lax.rem(z + 3, NZ)
    parity, level = lax.rem(z, 2), z // 2
    barrier = entry_signal(me, z)
    load_wo = pltpu.make_async_copy(wo_hbm, wo, alsem.at[0])
    load_wo.start()
    load_res = pltpu.make_async_copy(res_hbm.at[rows(z, OWN), :], res, alsem.at[1])
    load_res.start()
    load_g = pltpu.make_async_copy(gate_hbm.at[0], wgu.at[:, 0:SL], lsem.at[1])
    load_u = pltpu.make_async_copy(up_hbm.at[0], wgu.at[:, SL : 2 * SL], lsem.at[2])
    load_d = pltpu.make_async_copy(down_hbm.at[0], wd, lsem.at[3])
    for c in (load_g, load_u, load_d):
        c.start()

    starts = [jnp.int32(0)]
    for i in range(15):
        starts.append(starts[-1] + docs[i])

    def doc_at(pos):
        total = jnp.zeros(pos.shape, I32)
        for s in starts:
            total = total + (pos >= s).astype(I32)
        return total

    base = me * TOK
    t_col = lax.broadcasted_iota(I32, (TOK, 1), 0)
    t_row = lax.broadcasted_iota(I32, (1, TOK), 1)
    doc_col = doc_at(base + t_col)
    doc_row = doc_at(base + t_row)
    doc_first, doc_last = jnp.int32(0), jnp.int32(0)
    for s in starts:
        doc_first = doc_first + (base >= s).astype(I32)
        doc_last = doc_last + (base + TOK - 1 >= s).astype(I32)
    same_last = (doc_col == doc_last).astype(F32)
    same_first = (doc_col == doc_first).astype(F32)
    end_dist = (TOK - t_col).astype(F32)
    local_f = t_col.astype(F32)

    for h in range(HEADS):
        cols = slice(h * HS, (h + 1) * HS)
        w = jnp.exp(-rates[h] * end_dist) * same_last
        kw = (k_ref[:, cols].astype(F32) * w).astype(BF16)
        state = lax.dot_general(
            kw, v_ref[:, cols], (((0,), (0,)), ((), ())), preferred_element_type=F32
        )
        st_send[h * HS : (h + 1) * HS, :] = state.astype(BF16)

    entry_wait(barrier)
    own_st = pltpu.make_async_copy(st_send.at[rows(me, 32), :], st_recv.at[me], alsem.at[2])
    own_st.start()

    def send_state(d):
        j = lax.rem(me + d, NSEQ)
        return rcopy(
            st_send.at[rows(j, 32), :], st_recv.at[me], as1.at[d], ar1.at[me], (j, z)
        )

    @pl.loop(1, NSEQ)
    def _(d):
        send_state(d).start()

    lag = lax.broadcasted_iota(I32, (TOK, TOK), 0) - lax.broadcasted_iota(I32, (TOK, TOK), 1)
    allowed = (lag >= 0) & (doc_col == doc_row)
    lag_f = jnp.where(allowed, lag.astype(F32), 3e38)

    def inner(h):
        cols = slice(h * HS, (h + 1) * HS)
        scores = lax.dot_general(
            q_ref[:, cols], k_ref[:, cols], (((1,), (1,)), ((), ())), preferred_element_type=F32
        )
        probs = (scores * jnp.exp(-rates[h] * lag_f)).astype(BF16)
        inside[h] = jnp.dot(probs, v_ref[:, cols], preferred_element_type=F32)

    for h in range(6):
        inner(h)

    own_st.wait()

    @pl.loop(1, NSEQ)
    def _(d):
        j = lax.rem(me + d, NSEQ)
        rcopy(st_send.at[rows(j, 32), :], st_recv.at[j], as1.at[d], ar1.at[j], (j, z)).wait_recv()

    c_pos = lax.broadcasted_iota(I32, (NSEQ, HS), 0) * TOK
    d_here = doc_at(c_pos)
    u = (d_here == doc_at(c_pos - 1)).astype(F32)
    g = (d_here == doc_at(c_pos - TOK)).astype(F32)
    r_own = rates[me // (NSEQ // HEADS)]
    coef[0] = u
    coef[1] = g * jnp.exp(jnp.full((NSEQ, HS), -float(TOK), F32) * r_own)
    total = jnp.zeros((32, HS), F32)
    ca_send[0] = total.astype(BF16)
    for c in range(1, NSEQ):
        total = coef[1, c : c + 1, :] * total + coef[0, c : c + 1, :] * st_recv[c - 1].astype(F32)
        ca_send[c] = total.astype(BF16)

    own_ca = pltpu.make_async_copy(ca_send.at[me], ca_recv.at[me], alsem.at[3])
    own_ca.start()

    @pl.loop(1, NSEQ)
    def _(d):
        j = lax.rem(me + d, NSEQ)
        rcopy(ca_send.at[j], ca_recv.at[me], as2.at[d], ar2.at[me], (j, z)).start()

    for h in range(6, 8):
        inner(h)

    def rank_wanted(shape, axis):
        r = lax.broadcasted_iota(I32, shape, axis)
        return (parity * 8 + lax.rem(r // 8, 2) * 16 + lax.rem(r, 8)).astype(F32)

    def onehot(flag):
        return flag.astype(F32).astype(BF16)

    def flip(a):
        return lax.dot_general(a, eye, (((0,), (0,)), ((), ())), preferred_element_type=F32)

    e_sub = lax.broadcasted_iota(I32, (16, TOK), 0)
    one0_t = onehot(routes_t[0:1, :] == e_sub)
    one1_t = onehot(routes_t[1:2, :] == e_sub)
    chosen_t = one0_t + one1_t
    before_t = onehot(
        lax.broadcasted_iota(I32, (TOK, TOK), 0) < lax.broadcasted_iota(I32, (TOK, TOK), 1)
    )
    rank_t = jnp.dot(chosen_t, before_t, preferred_element_type=F32).astype(BF16)
    expand_t = onehot(
        lax.broadcasted_iota(I32, (TOK, 16), 0) // 16 == lax.broadcasted_iota(I32, (TOK, 16), 1)
    )
    rank_big = jnp.dot(expand_t, rank_t, preferred_element_type=F32)
    chosen_big = jnp.dot(expand_t, chosen_t, preferred_element_type=F32)
    pick[...] = jnp.where(rank_big == rank_wanted((TOK, 1), 0), chosen_big, 0.0).astype(BF16)
    eye = onehot(
        lax.broadcasted_iota(I32, (16, 16), 0) == lax.broadcasted_iota(I32, (16, 16), 1)
    )
    ones[0] = flip(one0_t)
    ones[1] = flip(one1_t)
    expand = onehot(
        lax.broadcasted_iota(I32, (16, TOK), 1) // 16 == lax.broadcasted_iota(I32, (16, TOK), 0)
    )
    rank_w = jnp.dot(flip(rank_t).astype(BF16), expand, preferred_element_type=F32)
    hit[...] = (rank_w == rank_wanted((1, TOK), 1)).astype(F32)

    own_ca.wait()

    @pl.loop(1, NSEQ)
    def _(d):
        j = lax.rem(me + d, NSEQ)
        rcopy(ca_send.at[j], ca_recv.at[j], as2.at[d], ar2.at[j], (j, z)).wait_recv()

    for h in range(HEADS):
        cols = slice(h * HS, (h + 1) * HS)
        carried = ca_recv[h * 4 : (h + 1) * 4].reshape(HS, HS)
        term = jnp.dot(q_ref[:, cols], carried, preferred_element_type=F32)
        raw = inside[h] + term * (jnp.exp(-rates[h] * local_f) * same_first)
        scale = lax.rsqrt(jnp.mean(raw * raw, axis=-1, keepdims=True) + EPSILON)
        attn[:, cols] = (raw * scale).astype(BF16)

    load_wo.wait()

    def project(h):
        p_ref[:, HALVES[h]] = jnp.dot(
            attn[...], wo[:, HALVES[h]], preferred_element_type=F32
        ).astype(BF16)

    share = reduce_scatter_z(me, z, project, p_ref, relay, acc, got, as3, ar3)
    load_res.wait()
    hidden = (res[...].astype(F32) + share).astype(BF16)
    kept[...] = hidden
    hid = hidden.astype(F32)
    scale = lax.rsqrt(jnp.mean(hid * hid, axis=-1, keepdims=True) + EPSILON)
    nbuf[rows(z, OWN), :] = (hid * scale).astype(BF16)
    all_gather_z(me, z, nbuf, as4, ar4)

    for n in range(D // 1024):
        cols = slice(n * 1024, (n + 1) * 1024)
        slots[:, cols] = jnp.dot(pick[...], nbuf[:, cols], preferred_element_type=F32).astype(BF16)

    def away(i, sign):
        m = lax.rem(i, 4)
        dx = lax.rem(2 * m, 4) + m // 2
        dy = lax.rem(i // 4 - dx + 4, 4)
        return lax.rem(cx + sign * dx + 4, 4) * 4 + lax.rem(cy + sign * dy + 4, 4)

    def span(start, size, align):
        return pl.ds(pl.multiple_of(start, align), size)

    def x_rows(st, i):
        i0, n = st
        return span(64 * i0 + core * 32 * n + parity * 16 * n + (i - i0) * 16, 16, 16)

    def x_unit(st, i, unit):
        i0, n = st
        r = 64 * i0 + core * 32 * n + lax.rem(unit, 2) * 16 * n + (i - i0) * 16
        return span(r + (unit // 2) * 8, 8, 8)

    def half(st, par):
        i0, n = st
        return span(64 * i0 + par * 32 * n, 32 * n, 32 * n)

    def b_all(st):
        i0, n = st
        return pl.ds(32 * i0, 32 * n)

    def b_rows(st, i):
        i0, n = st
        return span(32 * i0 + parity * 16 * n + (i - i0) * 16, 16, 16)

    def b_unit(st, i, unit):
        i0, n = st
        r = 32 * i0 + lax.rem(unit, 2) * 16 * n + (i - i0) * 16
        return span(r + (unit // 2) * 8, 8, 8)

    def loop_over(st, fn, skip=0):
        i0, n = st

        @pl.loop(i0 + skip, i0 + n)
        def _(i):
            fn(i)

    def send1(st, i):
        e = away(i, 1)
        return rcopy(
            slots.at[rows(e, 16), :],
            x.at[x_rows(st, i), :],
            s1.at[i],
            r1.at[i],
            (e * 2 + core, z),
        )

    own1 = pltpu.make_async_copy(
        slots.at[rows(chip, 16), :], x.at[x_rows(STAGES[0], 0), :], lsem.at[4]
    )
    own1.start()
    for st in STAGES:
        loop_over(st, lambda i: send1(st, i).start(), 1 if st[0] == 0 else 0)

    logits = lax.dot_general(
        nbuf[...], router_t[...], (((1,), (1,)), ((), ())), preferred_element_type=F32
    )
    one0, one1 = ones[0], ones[1]
    l0 = jnp.sum(one0 * logits, axis=1, keepdims=True)
    l1 = jnp.sum(one1 * logits, axis=1, keepdims=True)
    weight = one0 * jax.nn.sigmoid(l0 - l1) + one1 * jax.nn.sigmoid(l1 - l0)
    expand = onehot(
        lax.broadcasted_iota(I32, (16, TOK), 1) // 16 == lax.broadcasted_iota(I32, (16, TOK), 0)
    )
    weight_w = jnp.dot(weight.astype(BF16), expand, preferred_element_type=F32)
    mixw[...] = (weight_w * hit[...]).astype(BF16)

    for c in (load_g, load_u, load_d):
        c.wait()

    def pass_on(st, i, side):
        view = x.at[x_unit(st, i, z), :]
        to = up_z if side == 0 else down_z
        return rcopy(view, view, sz.at[i, side], rz.at[i, side], (me, to))

    def passed(st, i, side):
        view = x.at[x_unit(st, i, down_z if side == 0 else up_z), :]
        return rcopy(view, view, sz.at[i, side], rz.at[i, side], (me, up_z))

    def arrive(st):
        skip = 1 if st[0] == 0 else 0
        if skip:
            own1.wait()
            pass_on(st, 0, 0).start()
            pass_on(st, 0, 1).start()

        def one(i):
            view = x.at[x_rows(st, i), :]
            rcopy(view, view, s1.at[0], r1.at[i], partner).wait_recv()
            pass_on(st, i, 0).start()
            pass_on(st, i, 1).start()

        loop_over(st, one, skip)

    def hand(k, side):
        view = x.at[half(STAGES[k], side), :]
        return rcopy(view, view, s2.at[k], r2.at[k], partner)

    def hand_over(k):
        def one(i):
            passed(STAGES[k], i, 0).wait_recv()
            passed(STAGES[k], i, 1).wait_recv()

        loop_over(STAGES[k], one)
        hand(k, core).start()

    def pair(k, h):
        st = STAGES[k]
        return rcopy(
            y.at[half(st, other), HALVES[h]],
            y_recv.at[b_all(st), HALVES[h]],
            s3.at[k, h],
            r3.at[k, h],
            partner,
        )

    def z_back(st, i, side, h):
        unit = up_z if side == 0 else down_z
        return rcopy(
            back.at[b_unit(st, i, unit), HALVES[h]],
            z_recv.at[side, rows(i, 8), HALVES[h]],
            sq.at[i, side, h],
            rq.at[i, side, h],
            (me, unit),
        )

    def pair_sum(k, h):
        st, cols = STAGES[k], HALVES[h]
        pair(k, h).wait_recv()
        back[b_all(st), cols] = (
            y[half(st, core), cols].astype(F32) + y_recv[b_all(st), cols].astype(F32)
        ).astype(BF16)

        def one(i):
            z_back(st, i, 0, h).start()
            z_back(st, i, 1, h).start()

        loop_over(st, one)

    def send_back(st, i, h):
        return rcopy(
            back.at[b_rows(st, i), HALVES[h]],
            table.at[rows(chip, 16), HALVES[h]],
            s4.at[i, h],
            r4.at[i, h],
            (away(i, -1) * 2 + core, z),
        )

    def stay(h):
        return pltpu.make_async_copy(
            back.at[b_rows(STAGES[0], 0), HALVES[h]],
            table.at[rows(chip, 16), HALVES[h]],
            lsem.at[5 + h],
        )

    def z_sum(k, h):
        st, cols = STAGES[k], HALVES[h]

        def one(i):
            z_back(st, i, 0, h).wait_recv()
            z_back(st, i, 1, h).wait_recv()
            r = b_unit(st, i, z)
            back[r, cols] = (
                back[r, cols].astype(F32)
                + z_recv[0, rows(i, 8), cols].astype(F32)
                + z_recv[1, rows(i, 8), cols].astype(F32)
            ).astype(BF16)

        loop_over(st, one)
        skip = 1 if st[0] == 0 else 0
        if skip:
            stay(h).start()
        loop_over(st, lambda i: send_back(st, i, h).start(), skip)

    last = len(STAGES) - 1
    arrive(STAGES[0])
    arrive(STAGES[1])
    hand_over(0)
    for k, (i0, n) in enumerate(STAGES):
        m = 64 * n
        hand(k, other).wait_recv()
        hbuf[0:m, :] = jnp.dot(
            x[64 * i0 : 64 * i0 + m, :], wgu[...], preferred_element_type=F32
        )
        if k < last:
            hand_over(k + 1)
        if k + 1 < last:
            arrive(STAGES[k + 2])
        if k > 0:
            pair_sum(k - 1, 0)
            pair_sum(k - 1, 1)
        gate, up = hbuf[0:m, 0:SL], hbuf[0:m, SL : 2 * SL]
        abuf[0:m, :] = (gate * jax.nn.sigmoid(gate) * up).astype(BF16)
        if k > 1:
            z_sum(k - 2, 0)
            z_sum(k - 2, 1)
        for h in (0, 1):
            y[64 * i0 : 64 * i0 + m, HALVES[h]] = jnp.dot(
                abuf[0:m, :], wd[:, HALVES[h]], preferred_element_type=F32
            ).astype(BF16)
            pair(k, h).start()

    pair_sum(last, 0)
    z_sum(last - 1, 0)
    pair_sum(last, 1)
    z_sum(last - 1, 1)
    z_sum(last, 0)
    z_sum(last, 1)

    def mix(h):
        stay(h).wait()

        @pl.loop(1, 16)
        def _(i):
            view = table.at[rows(away(i, 1), 16), HALVES[h]]
            rcopy(view, view, s4.at[0, 0], r4.at[i, h], partner).wait_recv()

        p_ref[:, HALVES[h]] = jnp.dot(
            mixw[...], table[:, HALVES[h]], preferred_element_type=F32
        ).astype(BF16)

    share = reduce_scatter_z(me, z, mix, p_ref, relay2, acc2, got2, s5, r5)
    out_ref[...] = (kept[...].astype(F32) + share).astype(BF16)

    for k, st in enumerate(STAGES):
        hand(k, core).wait_send()
        pair(k, 0).wait_send()
        pair(k, 1).wait_send()
        skip = 1 if st[0] == 0 else 0

        def one(i):
            send1(st, i).wait_send()
            send_back(st, i, 0).wait_send()
            send_back(st, i, 1).wait_send()

        loop_over(st, one, skip)

        def two(i):
            for side in (0, 1):
                pass_on(st, i, side).wait_send()
                z_back(st, i, side, 0).wait_send()
                z_back(st, i, side, 1).wait_send()

        loop_over(st, two)

    @pl.loop(1, NSEQ)
    def _(d):
        j = lax.rem(me + d, NSEQ)
        send_state(d).wait_send()
        rcopy(ca_send.at[j], ca_recv.at[me], as2.at[d], ar2.at[me], (j, z)).wait_send()


VM = pl.BlockSpec(memory_space=pltpu.VMEM)
SM = pl.BlockSpec(memory_space=pltpu.SMEM)
HB = pl.BlockSpec(memory_space=pl.ANY)
DMA = pltpu.SemaphoreType.DMA
V = pltpu.VMEM

SCRATCH = (
    (
        V((HEADS * HS, D), BF16),
        V((OWN, D), BF16),
        V((HEADS * HS, HS), BF16),
        V((NSEQ, 32, HS), BF16),
        V((NSEQ, 32, HS), BF16),
        V((NSEQ, 32, HS), BF16),
        V((2, NSEQ, HS), F32),
        V((HEADS, TOK, HS), F32),
        V((TOK, HEADS * HS), BF16),
        V((OWN, D), BF16),
    ),
    (
        V((TOK, D), BF16),
        V((2, OWN, HALF), BF16),
        V((2, OWN, HALF), BF16),
        V((2, OWN, D), BF16),
        V((2, OWN, HALF), BF16),
        V((2, OWN, HALF), BF16),
        V((2, OWN, D), BF16),
    ),
    (
        V((TOK, D), BF16),
        V((D, 2 * SL), BF16),
        V((SL, D), BF16),
        V((TOK, TOK), BF16),
        V((2, TOK, 16), F32),
        V((TOK, TOK), F32),
        V((TOK, D), BF16),
        V((TOK, TOK), BF16),
        V((4 * TOK, D), BF16),
        V((TOK, 2 * SL), F32),
        V((TOK, SL), BF16),
        V((4 * TOK, D), BF16),
        V((2 * TOK, D), BF16),
        V((2 * TOK, D), BF16),
        V((2, 128, D), BF16),
        V((TOK, D), BF16),
    ),
    tuple(DMA((n,)) for n in (5, NSEQ, NSEQ, NSEQ, NSEQ, 6, 6, 6, 6)),
    (
        DMA((7,)),
        DMA((16,)),
        DMA((16,)),
        DMA((16, 2)),
        DMA((16, 2)),
        DMA((len(STAGES),)),
        DMA((len(STAGES),)),
        DMA((len(STAGES), 2)),
        DMA((len(STAGES), 2)),
        DMA((16, 2, 2)),
        DMA((16, 2, 2)),
        DMA((16, 2)),
        DMA((16, 2)),
        DMA((6,)),
        DMA((6,)),
    ),
)
SCRATCH_LIST, SCRATCH_TREE = jax.tree.flatten(SCRATCH)


def body(
    residual_in,
    queries,
    keys,
    values,
    rates,
    doc_lengths,
    out_weight,
    router,
    gate_weight,
    up_weight,
    down_weight,
    routes,
):
    return pl.pallas_call(
        layer_kernel,
        name="layer",
        out_shape=jax.ShapeDtypeStruct((OWN, D), BF16),
        in_specs=[SM, SM, VM, VM, VM, VM, VM, HB, HB, HB, HB, HB],
        out_specs=VM,
        scratch_shapes=SCRATCH_LIST,
        compiler_params=pltpu.CompilerParams(
            collective_id=0, has_side_effects=True, vmem_limit_bytes=VMEM_LIMIT
        ),
    )(
        rates,
        doc_lengths,
        queries,
        keys,
        values,
        routes.T,
        router.T,
        residual_in,
        out_weight,
        gate_weight,
        up_weight,
        down_weight,
    )


def solution(mesh):
    in_specs = (
        P("seq", None),
        P("seq", "exp"),
        P("seq", "exp"),
        P("seq", "exp"),
        P("exp"),
        P(),
        P("exp", None),
        P(),
        P("seq", None, "exp"),
        P("seq", None, "exp"),
        P("seq", "exp", None),
        P("seq", None),
    )
    out_specs = P(("seq", "exp"), None)
    return jax.shard_map(body, mesh=mesh, in_specs=in_specs, out_specs=out_specs, check_vma=False)
```

```python
import functools

import jax
import jax.numpy as jnp
from jax import lax
from jax.experimental import pallas as pl
from jax.experimental.pallas import tpu as pltpu
from jax.sharding import PartitionSpec as P

EPSILON = 1e-06
MESH = pl.DeviceIdType.MESH
F32, BF16, I32 = jnp.float32, jnp.bfloat16, jnp.int32
NSEQ, NZ = 32, 4
TOK, D, HEADS, HS = 256, 3072, 8, 128
OWN = TOK // NZ
HALF = D // 2
SL = 640
VMEM_LIMIT = 63_000_000
STAGES = ((0, 4), (4, 4), (8, 4), (12, 4))


def rcopy(src, dst, ssem, rsem, dev):
    return pltpu.make_async_remote_copy(
        src_ref=src, dst_ref=dst, send_sem=ssem, recv_sem=rsem, device_id=dev, device_id_type=MESH
    )


def rows(r, n):
    return pl.ds(pl.multiple_of(r * n, n), n)


def entry_signal(me, z):
    barrier = pltpu.get_barrier_semaphore()

    @pl.loop(1, NSEQ)
    def _(d):
        pl.semaphore_signal(
            barrier, inc=1, device_id=(lax.rem(me + d, NSEQ), z), device_id_type=MESH
        )

    for dz in (1, 3):
        pl.semaphore_signal(
            barrier, inc=1, device_id=(me, lax.rem(z + dz, NZ)), device_id_type=MESH
        )
    return barrier


def entry_wait(barrier):
    pl.semaphore_wait(barrier, NSEQ + 1)


A = slice(0, HALF)
B = slice(HALF, D)
HALVES = (A, B)
WIDE = D + 128
XC = (slice(0, HALF), slice(HALF, WIDE))
QUART = D // 4


def reduce_scatter_z(me, z, make, p_ref, relay, acc, got, ssem, rsem):
    right, left, far = lax.rem(z + 1, NZ), lax.rem(z + 3, NZ), lax.rem(z + 2, NZ)
    dr, dl = (me, right), (me, left)
    c1 = rcopy(p_ref.at[rows(far, OWN), A], relay.at[0], ssem.at[0], rsem.at[0], dr)
    c2 = rcopy(p_ref.at[rows(far, OWN), B], relay.at[1], ssem.at[1], rsem.at[1], dl)
    c3 = rcopy(p_ref.at[rows(right, OWN), B], got.at[0, :, B], ssem.at[2], rsem.at[2], dr)
    c4 = rcopy(p_ref.at[rows(left, OWN), A], got.at[1, :, A], ssem.at[3], rsem.at[3], dl)
    make(0)
    c1.start()
    c4.start()
    make(1)
    c2.start()
    c3.start()
    c1.wait_recv()
    acc[0] = (p_ref[rows(right, OWN), A].astype(F32) + relay[0].astype(F32)).astype(BF16)
    c5 = rcopy(acc.at[0], got.at[0, :, A], ssem.at[4], rsem.at[4], dr)
    c5.start()
    c2.wait_recv()
    acc[1] = (p_ref[rows(left, OWN), B].astype(F32) + relay[1].astype(F32)).astype(BF16)
    c6 = rcopy(acc.at[1], got.at[1, :, B], ssem.at[5], rsem.at[5], dl)
    c6.start()
    for c in (c3, c4, c5, c6):
        c.wait_recv()
    total = (
        p_ref[rows(z, OWN), :].astype(F32) + got[0].astype(F32) + got[1].astype(F32)
    )
    for c in (c1, c2, c3, c4, c5, c6):
        c.wait_send()
    return total


def layer_kernel(
    rates,
    docs,
    q_ref,
    k_ref,
    v_ref,
    routes_t,
    router_t,
    res_hbm,
    wo_hbm,
    gate_hbm,
    up_hbm,
    down_hbm,
    out_ref,
    *scratch,
):
    (
        (wo, res, st_send, st_recv, ca_send, ca_recv, coef, inside, attn, kept),
        (p_ref, relay, acc, got, relay2, acc2, got2),
        (nbuf, wgu, wd, pick, ones, hit, slots, mixw, x, hbuf, abuf, y, y_recv, back, z_recv, table),
        (alsem, as1, ar1, as2, ar2, as3, ar3, as4, ar4),
        (lsem, s1, r1, sz, rz, s2, r2, s3, r3, sq, rq, s4, r4, s5, r5),
    ) = jax.tree.unflatten(SCRATCH_TREE, scratch)
    me, z = lax.axis_index("seq"), lax.axis_index("exp")
    chip, core = me // 2, lax.rem(me, 2)
    other = 1 - core
    cx, cy = chip // 4, lax.rem(chip, 4)
    partner = (chip * 2 + other, z)
    up_z, down_z = lax.rem(z + 1, NZ), lax.rem(z + 3, NZ)
    parity, level = lax.rem(z, 2), z // 2
    barrier = entry_signal(me, z)
    load_wo = pltpu.make_async_copy(wo_hbm, wo, alsem.at[0])
    load_wo.start()
    load_res = pltpu.make_async_copy(res_hbm.at[rows(z, OWN), :], res, alsem.at[1])
    load_res.start()
    load_g = pltpu.make_async_copy(gate_hbm.at[0], wgu.at[:, 0:SL], lsem.at[1])
    load_u = pltpu.make_async_copy(up_hbm.at[0], wgu.at[:, SL : 2 * SL], lsem.at[2])
    load_d = pltpu.make_async_copy(down_hbm.at[0], wd, lsem.at[3])
    for c in (load_g, load_u, load_d):
        c.start()

    starts = [jnp.int32(0)]
    for i in range(15):
        starts.append(starts[-1] + docs[i])

    def doc_at(pos):
        total = jnp.zeros(pos.shape, I32)
        for s in starts:
            total = total + (pos >= s).astype(I32)
        return total

    base = me * TOK
    t_col = lax.broadcasted_iota(I32, (TOK, 1), 0)
    t_row = lax.broadcasted_iota(I32, (1, TOK), 1)
    doc_col = doc_at(base + t_col)
    doc_row = doc_at(base + t_row)
    doc_first, doc_last = jnp.int32(0), jnp.int32(0)
    for s in starts:
        doc_first = doc_first + (base >= s).astype(I32)
        doc_last = doc_last + (base + TOK - 1 >= s).astype(I32)
    same_last = (doc_col == doc_last).astype(F32)
    same_first = (doc_col == doc_first).astype(F32)
    end_dist = (TOK - t_col).astype(F32)
    local_f = t_col.astype(F32)

    for h in range(HEADS):
        cols = slice(h * HS, (h + 1) * HS)
        w = jnp.exp(-rates[h] * end_dist) * same_last
        kw = (k_ref[:, cols].astype(F32) * w).astype(BF16)
        state = lax.dot_general(
            kw, v_ref[:, cols], (((0,), (0,)), ((), ())), preferred_element_type=F32
        )
        st_send[h * HS : (h + 1) * HS, :] = state.astype(BF16)

    entry_wait(barrier)
    own_st = pltpu.make_async_copy(st_send.at[rows(me, 32), :], st_recv.at[me], alsem.at[2])
    own_st.start()

    def send_state(d):
        j = lax.rem(me + d, NSEQ)
        return rcopy(
            st_send.at[rows(j, 32), :], st_recv.at[me], as1.at[d], ar1.at[me], (j, z)
        )

    @pl.loop(1, NSEQ)
    def _(d):
        send_state(d).start()

    lag = lax.broadcasted_iota(I32, (TOK, TOK), 0) - lax.broadcasted_iota(I32, (TOK, TOK), 1)
    allowed = (lag >= 0) & (doc_col == doc_row)
    lag_f = jnp.where(allowed, lag.astype(F32), 3e38)

    def inner(h):
        cols = slice(h * HS, (h + 1) * HS)
        scores = lax.dot_general(
            q_ref[:, cols], k_ref[:, cols], (((1,), (1,)), ((), ())), preferred_element_type=F32
        )
        probs = (scores * jnp.exp(-rates[h] * lag_f)).astype(BF16)
        inside[h] = jnp.dot(probs, v_ref[:, cols], preferred_element_type=F32)

    for h in range(6):
        inner(h)

    own_st.wait()

    @pl.loop(1, NSEQ)
    def _(d):
        j = lax.rem(me + d, NSEQ)
        rcopy(st_send.at[rows(j, 32), :], st_recv.at[j], as1.at[d], ar1.at[j], (j, z)).wait_recv()

    c_pos = lax.broadcasted_iota(I32, (NSEQ, HS), 0) * TOK
    d_here = doc_at(c_pos)
    u = (d_here == doc_at(c_pos - 1)).astype(F32)
    g = (d_here == doc_at(c_pos - TOK)).astype(F32)
    r_own = rates[me // (NSEQ // HEADS)]
    coef[0] = u
    coef[1] = g * jnp.exp(jnp.full((NSEQ, HS), -float(TOK), F32) * r_own)
    total = jnp.zeros((32, HS), F32)
    ca_send[0] = total.astype(BF16)
    for c in range(1, NSEQ):
        total = coef[1, c : c + 1, :] * total + coef[0, c : c + 1, :] * st_recv[c - 1].astype(F32)
        ca_send[c] = total.astype(BF16)

    own_ca = pltpu.make_async_copy(ca_send.at[me], ca_recv.at[me], alsem.at[3])
    own_ca.start()

    @pl.loop(1, NSEQ)
    def _(d):
        j = lax.rem(me + d, NSEQ)
        rcopy(ca_send.at[j], ca_recv.at[me], as2.at[d], ar2.at[me], (j, z)).start()

    for h in range(6, 8):
        inner(h)

    def rank_wanted(shape, axis):
        r = lax.broadcasted_iota(I32, shape, axis)
        return (parity * 8 + lax.rem(r // 8, 2) * 16 + lax.rem(r, 8)).astype(F32)

    def onehot(flag):
        return flag.astype(F32).astype(BF16)

    def flip(a):
        return lax.dot_general(a, eye, (((0,), (0,)), ((), ())), preferred_element_type=F32)

    e_sub = lax.broadcasted_iota(I32, (16, TOK), 0)
    one0_t = onehot(routes_t[0:1, :] == e_sub)
    one1_t = onehot(routes_t[1:2, :] == e_sub)
    chosen_t = one0_t + one1_t
    before_t = onehot(
        lax.broadcasted_iota(I32, (TOK, TOK), 0) < lax.broadcasted_iota(I32, (TOK, TOK), 1)
    )
    rank_t = jnp.dot(chosen_t, before_t, preferred_element_type=F32).astype(BF16)
    expand_t = onehot(
        lax.broadcasted_iota(I32, (TOK, 16), 0) // 16 == lax.broadcasted_iota(I32, (TOK, 16), 1)
    )
    rank_big = jnp.dot(expand_t, rank_t, preferred_element_type=F32)
    chosen_big = jnp.dot(expand_t, chosen_t, preferred_element_type=F32)
    pick[...] = jnp.where(rank_big == rank_wanted((TOK, 1), 0), chosen_big, 0.0).astype(BF16)
    eye = onehot(
        lax.broadcasted_iota(I32, (16, 16), 0) == lax.broadcasted_iota(I32, (16, 16), 1)
    )
    ones[0] = flip(one0_t)
    ones[1] = flip(one1_t)
    expand = onehot(
        lax.broadcasted_iota(I32, (16, TOK), 1) // 16 == lax.broadcasted_iota(I32, (16, TOK), 0)
    )
    rank_w = jnp.dot(flip(rank_t).astype(BF16), expand, preferred_element_type=F32)
    hit[...] = (rank_w == rank_wanted((1, TOK), 1)).astype(F32)

    own_ca.wait()

    @pl.loop(1, NSEQ)
    def _(d):
        j = lax.rem(me + d, NSEQ)
        rcopy(ca_send.at[j], ca_recv.at[j], as2.at[d], ar2.at[j], (j, z)).wait_recv()

    for h in range(HEADS):
        cols = slice(h * HS, (h + 1) * HS)
        carried = ca_recv[h * 4 : (h + 1) * 4].reshape(HS, HS)
        term = jnp.dot(q_ref[:, cols], carried, preferred_element_type=F32)
        raw = inside[h] + term * (jnp.exp(-rates[h] * local_f) * same_first)
        scale = lax.rsqrt(jnp.mean(raw * raw, axis=-1, keepdims=True) + EPSILON)
        attn[:, cols] = (raw * scale).astype(BF16)

    load_wo.wait()

    def project(h):
        p_ref[:, HALVES[h]] = jnp.dot(
            attn[...], wo[:, HALVES[h]], preferred_element_type=F32
        ).astype(BF16)

    right, left, far = lax.rem(z + 1, NZ), lax.rem(z + 3, NZ), lax.rem(z + 2, NZ)
    dr, dl = (me, right), (me, left)

    def quarters(h):
        return (
            slice(h * HALF, h * HALF + QUART),
            slice(h * HALF + QUART, (h + 1) * HALF),
        )

    def rs(h):
        qa, qb = quarters(h)

        def go(j, src, dst, dev):
            return rcopy(src, dst, as3.at[h, j], ar3.at[h, j], dev)

        return (
            go(0, p_ref.at[rows(far, OWN), qa], relay.at[h, 0], dr),
            go(1, p_ref.at[rows(far, OWN), qb], relay.at[h, 1], dl),
            go(2, p_ref.at[rows(right, OWN), qb], got.at[0, :, qb], dr),
            go(3, p_ref.at[rows(left, OWN), qa], got.at[1, :, qa], dl),
            go(4, acc.at[h, 0], got.at[0, :, qa], dr),
            go(5, acc.at[h, 1], got.at[1, :, qb], dl),
        )

    def ag(h):
        qa, qb = quarters(h)

        def go(j, owner, cols, dev):
            view = nbuf.at[rows(owner, OWN), cols]
            return rcopy(view, view, as4.at[h, j], ar4.at[h, j], dev)

        return (
            go(0, z, qa, dr),
            go(1, z, qb, dl),
            go(2, z, qb, dr),
            go(3, z, qa, dl),
            go(4, left, qa, dr),
            go(5, right, qb, dl),
        )

    def first_sends(c):
        for j in (0, 3, 1, 2):
            c[j].start()

    def rs_relay(h):
        qa, qb = quarters(h)
        c = rs_copies[h]
        c[0].wait_recv()
        acc[h, 0] = (
            p_ref[rows(right, OWN), qa].astype(F32) + relay[h, 0].astype(F32)
        ).astype(BF16)
        c[4].start()
        c[1].wait_recv()
        acc[h, 1] = (p_ref[rows(left, OWN), qb].astype(F32) + relay[h, 1].astype(F32)).astype(BF16)
        c[5].start()

    def rs_end(h):
        for j in (2, 3, 4, 5):
            rs_copies[h][j].wait_recv()
        cols = HALVES[h]
        share = (
            p_ref[rows(z, OWN), cols].astype(F32)
            + got[0, :, cols].astype(F32)
            + got[1, :, cols].astype(F32)
        )
        hidden = (res[:, cols].astype(F32) + share).astype(BF16)
        kept[:, cols] = hidden
        nbuf[rows(z, OWN), cols] = hidden
        first_sends(ag_copies[h])

    def ag_relay(h):
        c = ag_copies[h]
        c[0].wait_recv()
        c[4].start()
        c[1].wait_recv()
        c[5].start()

    def ag_end(h):
        for j in (2, 3, 4, 5):
            ag_copies[h][j].wait_recv()

    def squares(h):
        part = nbuf[:, HALVES[h]].astype(F32)
        return jnp.sum(part * part, axis=-1, keepdims=True)

    rs_copies, ag_copies = (rs(0), rs(1)), (ag(0), ag(1))
    project(0)
    first_sends(rs_copies[0])
    project(1)
    rs_relay(0)
    first_sends(rs_copies[1])
    load_res.wait()
    rs_end(0)
    rs_relay(1)
    ag_relay(0)
    rs_end(1)
    ag_end(0)

    def away(i, sign):
        m = lax.rem(i, 4)
        dx = lax.rem(2 * m, 4) + m // 2
        dy = lax.rem(i // 4 - dx + 4, 4)
        return lax.rem(cx + sign * dx + 4, 4) * 4 + lax.rem(cy + sign * dy + 4, 4)

    def span(start, size, align):
        return pl.ds(pl.multiple_of(start, align), size)

    def x_rows(st, i):
        i0, n = st
        return span(64 * i0 + core * 32 * n + parity * 16 * n + (i - i0) * 16, 16, 16)

    def x_unit(st, i, unit):
        i0, n = st
        r = 64 * i0 + core * 32 * n + lax.rem(unit, 2) * 16 * n + (i - i0) * 16
        return span(r + (unit // 2) * 8, 8, 8)

    def half(st, par):
        i0, n = st
        return span(64 * i0 + par * 32 * n, 32 * n, 32 * n)

    def b_all(st):
        i0, n = st
        return pl.ds(32 * i0, 32 * n)

    def b_rows(st, i):
        i0, n = st
        return span(32 * i0 + parity * 16 * n + (i - i0) * 16, 16, 16)

    def b_unit(st, i, unit):
        i0, n = st
        r = 32 * i0 + lax.rem(unit, 2) * 16 * n + (i - i0) * 16
        return span(r + (unit // 2) * 8, 8, 8)

    def loop_over(st, fn, skip=0):
        i0, n = st

        @pl.loop(i0 + skip, i0 + n)
        def _(i):
            fn(i)

    def send1(st, i, h):
        e = away(i, 1)
        return rcopy(
            slots.at[rows(e, 16), XC[h]],
            x.at[x_rows(st, i), XC[h]],
            s1.at[i, h],
            r1.at[i, h],
            (e * 2 + core, z),
        )

    def keep1(h):
        return pltpu.make_async_copy(
            slots.at[rows(chip, 16), XC[h]],
            x.at[x_rows(STAGES[0], 0), XC[h]],
            lsem.at[7 + h],
        )

    def dispatch(h):
        slots[:, XC[h]] = jnp.dot(
            pick[...], nbuf[:, XC[h]], preferred_element_type=F32
        ).astype(BF16)
        keep1(h).start()
        for st in STAGES:
            loop_over(st, lambda i: send1(st, i, h).start(), 1 if st[0] == 0 else 0)

    dispatch(0)
    square_sum = squares(0)
    ag_relay(1)
    ag_end(1)
    scale = lax.rsqrt((square_sum + squares(1)) * (1.0 / D) + EPSILON)
    high = scale.astype(BF16).astype(F32)
    lane = lax.broadcasted_iota(I32, (TOK, 128), 1)
    nbuf[:, D:WIDE] = jnp.where(
        lane == 0, high, jnp.where(lane == 1, scale - high, 0.0)
    ).astype(BF16)
    dispatch(1)

    for c in (load_g, load_u, load_d):
        c.wait()

    def pass_on(st, i, side, h):
        view = x.at[x_unit(st, i, z), XC[h]]
        to = up_z if side == 0 else down_z
        return rcopy(view, view, sz.at[i, side, h], rz.at[i, side, h], (me, to))

    def passed(st, i, side, h):
        view = x.at[x_unit(st, i, down_z if side == 0 else up_z), XC[h]]
        return rcopy(view, view, sz.at[i, side, h], rz.at[i, side, h], (me, up_z))

    def arrive(k, h):
        st = STAGES[k]
        skip = 1 if st[0] == 0 else 0
        if skip:
            keep1(h).wait()
            pass_on(st, 0, 0, h).start()
            pass_on(st, 0, 1, h).start()

        def one(i):
            view = x.at[x_rows(st, i), XC[h]]
            rcopy(view, view, s1.at[0, 0], r1.at[i, h], partner).wait_recv()
            pass_on(st, i, 0, h).start()
            pass_on(st, i, 1, h).start()

        loop_over(st, one, skip)

    def hand(k, side, h):
        view = x.at[half(STAGES[k], side), XC[h]]
        return rcopy(view, view, s2.at[k, h], r2.at[k, h], partner)

    def hand_over(k, h):
        def one(i):
            passed(STAGES[k], i, 0, h).wait_recv()
            passed(STAGES[k], i, 1, h).wait_recv()

        loop_over(STAGES[k], one)
        hand(k, core, h).start()

    def pair(k, h):
        st = STAGES[k]
        return rcopy(
            y.at[half(st, other), HALVES[h]],
            y_recv.at[b_all(st), HALVES[h]],
            s3.at[k, h],
            r3.at[k, h],
            partner,
        )

    def z_back(st, i, side, h):
        unit = up_z if side == 0 else down_z
        return rcopy(
            back.at[b_unit(st, i, unit), HALVES[h]],
            z_recv.at[side, rows(i, 8), HALVES[h]],
            sq.at[i, side, h],
            rq.at[i, side, h],
            (me, unit),
        )

    def pair_sum(k, h):
        st, cols = STAGES[k], HALVES[h]
        pair(k, h).wait_recv()
        back[b_all(st), cols] = (
            y[half(st, core), cols].astype(F32) + y_recv[b_all(st), cols].astype(F32)
        ).astype(BF16)

        def one(i):
            z_back(st, i, 0, h).start()
            z_back(st, i, 1, h).start()

        loop_over(st, one)

    def send_back(st, i, h):
        return rcopy(
            back.at[b_rows(st, i), HALVES[h]],
            table.at[rows(chip, 16), HALVES[h]],
            s4.at[i, h],
            r4.at[i, h],
            (away(i, -1) * 2 + core, z),
        )

    def stay(h):
        return pltpu.make_async_copy(
            back.at[b_rows(STAGES[0], 0), HALVES[h]],
            table.at[rows(chip, 16), HALVES[h]],
            lsem.at[5 + h],
        )

    def z_sum(k, h):
        st, cols = STAGES[k], HALVES[h]

        def one(i):
            z_back(st, i, 0, h).wait_recv()
            z_back(st, i, 1, h).wait_recv()
            r = b_unit(st, i, z)
            back[r, cols] = (
                back[r, cols].astype(F32)
                + z_recv[0, rows(i, 8), cols].astype(F32)
                + z_recv[1, rows(i, 8), cols].astype(F32)
            ).astype(BF16)

        loop_over(st, one)
        skip = 1 if st[0] == 0 else 0
        if skip:
            stay(h).start()
        loop_over(st, lambda i: send_back(st, i, h).start(), skip)

    last = len(STAGES) - 1

    def first_half(k):
        hand(k, other, 0).wait_recv()
        r = slice(256 * k, 256 * (k + 1))
        hbuf[r, :] = jnp.dot(x[r, XC[0]], wgu[0:HALF, :], preferred_element_type=F32)

    arrive(0, 0)
    arrive(1, 0)
    arrive(2, 0)
    hand_over(0, 0)
    arrive(3, 0)
    hand_over(1, 0)
    first_half(0)
    arrive(0, 1)
    hand_over(2, 0)
    first_half(1)
    arrive(1, 1)
    hand_over(3, 0)
    first_half(2)
    hand_over(0, 1)
    first_half(3)
    for k, (i0, n) in enumerate(STAGES):
        m = 64 * n
        r = slice(64 * i0, 64 * i0 + m)
        hand(k, other, 1).wait_recv()
        hbuf[r, :] += jnp.dot(x[r, HALF:D], wgu[HALF:D, :], preferred_element_type=F32)
        if k < last:
            hand_over(k + 1, 1)
        if k + 1 < last:
            arrive(k + 2, 1)
        if k > 0:
            pair_sum(k - 1, 0)
            pair_sum(k - 1, 1)
        parts = x[r, D:WIDE].astype(F32)
        row_scale = parts[:, 0:1] + parts[:, 1:2]
        gate, up = hbuf[r, 0:SL] * row_scale, hbuf[r, SL : 2 * SL] * row_scale
        abuf[0:m, :] = (gate * jax.nn.sigmoid(gate) * up).astype(BF16)
        for h in (0, 1):
            y[64 * i0 : 64 * i0 + m, HALVES[h]] = jnp.dot(
                abuf[0:m, :], wd[:, HALVES[h]], preferred_element_type=F32
            ).astype(BF16)
            pair(k, h).start()
            if k > 1:
                z_sum(k - 2, h)

    for h in (0, 1):
        for c in (*rs_copies[h], *ag_copies[h]):
            c.wait_send()

    logits = scale * lax.dot_general(
        nbuf[:, 0:D], router_t[...], (((1,), (1,)), ((), ())), preferred_element_type=F32
    )
    one0, one1 = ones[0], ones[1]
    l0 = jnp.sum(one0 * logits, axis=1, keepdims=True)
    l1 = jnp.sum(one1 * logits, axis=1, keepdims=True)
    weight = one0 * jax.nn.sigmoid(l0 - l1) + one1 * jax.nn.sigmoid(l1 - l0)
    expand = onehot(
        lax.broadcasted_iota(I32, (16, TOK), 1) // 16 == lax.broadcasted_iota(I32, (16, TOK), 0)
    )
    weight_w = jnp.dot(weight.astype(BF16), expand, preferred_element_type=F32)
    mixw[...] = (weight_w * hit[...]).astype(BF16)

    pair_sum(last, 0)
    z_sum(last - 1, 0)
    pair_sum(last, 1)
    z_sum(last - 1, 1)
    z_sum(last, 0)
    z_sum(last, 1)

    def mix(h):
        stay(h).wait()

        @pl.loop(1, 16)
        def _(i):
            view = table.at[rows(away(i, 1), 16), HALVES[h]]
            rcopy(view, view, s4.at[0, 0], r4.at[i, h], partner).wait_recv()

        p_ref[:, HALVES[h]] = jnp.dot(
            mixw[...], table[:, HALVES[h]], preferred_element_type=F32
        ).astype(BF16)

    share = reduce_scatter_z(me, z, mix, p_ref, relay2, acc2, got2, s5, r5)
    out_ref[...] = (kept[...].astype(F32) + share).astype(BF16)

    for k, st in enumerate(STAGES):
        hand(k, core, 0).wait_send()
        hand(k, core, 1).wait_send()
        pair(k, 0).wait_send()
        pair(k, 1).wait_send()
        skip = 1 if st[0] == 0 else 0

        def one(i):
            send1(st, i, 0).wait_send()
            send1(st, i, 1).wait_send()
            send_back(st, i, 0).wait_send()
            send_back(st, i, 1).wait_send()

        loop_over(st, one, skip)

        def two(i):
            for side in (0, 1):
                pass_on(st, i, side, 0).wait_send()
                pass_on(st, i, side, 1).wait_send()
                z_back(st, i, side, 0).wait_send()
                z_back(st, i, side, 1).wait_send()

        loop_over(st, two)

    @pl.loop(1, NSEQ)
    def _(d):
        j = lax.rem(me + d, NSEQ)
        send_state(d).wait_send()
        rcopy(ca_send.at[j], ca_recv.at[me], as2.at[d], ar2.at[me], (j, z)).wait_send()


VM = pl.BlockSpec(memory_space=pltpu.VMEM)
SM = pl.BlockSpec(memory_space=pltpu.SMEM)
HB = pl.BlockSpec(memory_space=pl.ANY)
DMA = pltpu.SemaphoreType.DMA
V = pltpu.VMEM

SCRATCH = (
    (
        V((HEADS * HS, D), BF16),
        V((OWN, D), BF16),
        V((HEADS * HS, HS), BF16),
        V((NSEQ, 32, HS), BF16),
        V((NSEQ, 32, HS), BF16),
        V((NSEQ, 32, HS), BF16),
        V((2, NSEQ, HS), F32),
        V((HEADS, TOK, HS), F32),
        V((TOK, HEADS * HS), BF16),
        V((OWN, D), BF16),
    ),
    (
        V((TOK, D), BF16),
        V((2, 2, OWN, QUART), BF16),
        V((2, 2, OWN, QUART), BF16),
        V((2, OWN, D), BF16),
        V((2, OWN, HALF), BF16),
        V((2, OWN, HALF), BF16),
        V((2, OWN, D), BF16),
    ),
    (
        V((TOK, WIDE), BF16),
        V((D, 2 * SL), BF16),
        V((SL, D), BF16),
        V((TOK, TOK), BF16),
        V((2, TOK, 16), F32),
        V((TOK, TOK), F32),
        V((TOK, WIDE), BF16),
        V((TOK, TOK), BF16),
        V((4 * TOK, WIDE), BF16),
        V((4 * TOK, 2 * SL), F32),
        V((TOK, SL), BF16),
        V((4 * TOK, D), BF16),
        V((2 * TOK, D), BF16),
        V((2 * TOK, D), BF16),
        V((2, 128, D), BF16),
        V((TOK, D), BF16),
    ),
    tuple(DMA((n,)) for n in (5, NSEQ, NSEQ, NSEQ, NSEQ)) + tuple(DMA((2, 6)) for _ in range(4)),
    (
        DMA((9,)),
        DMA((16, 2)),
        DMA((16, 2)),
        DMA((16, 2, 2)),
        DMA((16, 2, 2)),
        DMA((len(STAGES), 2)),
        DMA((len(STAGES), 2)),
        DMA((len(STAGES), 2)),
        DMA((len(STAGES), 2)),
        DMA((16, 2, 2)),
        DMA((16, 2, 2)),
        DMA((16, 2)),
        DMA((16, 2)),
        DMA((6,)),
        DMA((6,)),
    ),
)
SCRATCH_LIST, SCRATCH_TREE = jax.tree.flatten(SCRATCH)


def body(
    residual_in,
    queries,
    keys,
    values,
    rates,
    doc_lengths,
    out_weight,
    router,
    gate_weight,
    up_weight,
    down_weight,
    routes,
):
    return pl.pallas_call(
        layer_kernel,
        name="layer",
        out_shape=jax.ShapeDtypeStruct((OWN, D), BF16),
        in_specs=[SM, SM, VM, VM, VM, VM, VM, HB, HB, HB, HB, HB],
        out_specs=VM,
        scratch_shapes=SCRATCH_LIST,
        compiler_params=pltpu.CompilerParams(
            collective_id=0, has_side_effects=True, vmem_limit_bytes=VMEM_LIMIT
        ),
    )(
        rates,
        doc_lengths,
        queries,
        keys,
        values,
        routes.T,
        router.T,
        residual_in,
        out_weight,
        gate_weight,
        up_weight,
        down_weight,
    )


def solution(mesh):
    in_specs = (
        P("seq", None),
        P("seq", "exp"),
        P("seq", "exp"),
        P("seq", "exp"),
        P("exp"),
        P(),
        P("exp", None),
        P(),
        P("seq", None, "exp"),
        P("seq", None, "exp"),
        P("seq", "exp", None),
        P("seq", None),
    )
    out_specs = P(("seq", "exp"), None)
    return jax.shard_map(body, mesh=mesh, in_specs=in_specs, out_specs=out_specs, check_vma=False)
```

```python
import functools

import jax
import jax.numpy as jnp
from jax import lax
from jax.experimental import pallas as pl
from jax.experimental.pallas import tpu as pltpu
from jax.sharding import PartitionSpec as P

EPSILON = 1e-06
MESH = pl.DeviceIdType.MESH
F32, BF16, I32 = jnp.float32, jnp.bfloat16, jnp.int32
NSEQ, NZ = 32, 4
TOK, D, HEADS, HS = 256, 3072, 8, 128
OWN = TOK // NZ
HALF = D // 2
SL = 640
VMEM_LIMIT = 63_000_000
STAGES = ((0, 4), (4, 4), (8, 4), (12, 4))


def rcopy(src, dst, ssem, rsem, dev):
    return pltpu.make_async_remote_copy(
        src_ref=src, dst_ref=dst, send_sem=ssem, recv_sem=rsem, device_id=dev, device_id_type=MESH
    )


def rows(r, n):
    return pl.ds(pl.multiple_of(r * n, n), n)


def entry_signal(me, z):
    barrier = pltpu.get_barrier_semaphore()

    @pl.loop(1, NSEQ)
    def _(d):
        pl.semaphore_signal(
            barrier, inc=1, device_id=(lax.rem(me + d, NSEQ), z), device_id_type=MESH
        )

    for dz in (1, 3):
        pl.semaphore_signal(
            barrier, inc=1, device_id=(me, lax.rem(z + dz, NZ)), device_id_type=MESH
        )
    return barrier


def entry_wait(barrier):
    pl.semaphore_wait(barrier, NSEQ + 1)


A = slice(0, HALF)
B = slice(HALF, D)
HALVES = (A, B)
WIDE = D + 128
XC = (slice(0, HALF), slice(HALF, WIDE))
QUART = D // 4


def reduce_scatter_z(me, z, make, p_ref, relay, acc, got, ssem, rsem):
    right, left, far = lax.rem(z + 1, NZ), lax.rem(z + 3, NZ), lax.rem(z + 2, NZ)
    dr, dl = (me, right), (me, left)
    c1 = rcopy(p_ref.at[rows(far, OWN), A], relay.at[0], ssem.at[0], rsem.at[0], dr)
    c2 = rcopy(p_ref.at[rows(far, OWN), B], relay.at[1], ssem.at[1], rsem.at[1], dl)
    c3 = rcopy(p_ref.at[rows(right, OWN), B], got.at[0, :, B], ssem.at[2], rsem.at[2], dr)
    c4 = rcopy(p_ref.at[rows(left, OWN), A], got.at[1, :, A], ssem.at[3], rsem.at[3], dl)
    make(0)
    c1.start()
    c4.start()
    make(1)
    c2.start()
    c3.start()
    c1.wait_recv()
    acc[0] = (p_ref[rows(right, OWN), A].astype(F32) + relay[0].astype(F32)).astype(BF16)
    c5 = rcopy(acc.at[0], got.at[0, :, A], ssem.at[4], rsem.at[4], dr)
    c5.start()
    c2.wait_recv()
    acc[1] = (p_ref[rows(left, OWN), B].astype(F32) + relay[1].astype(F32)).astype(BF16)
    c6 = rcopy(acc.at[1], got.at[1, :, B], ssem.at[5], rsem.at[5], dl)
    c6.start()
    for c in (c3, c4, c5, c6):
        c.wait_recv()
    total = (
        p_ref[rows(z, OWN), :].astype(F32) + got[0].astype(F32) + got[1].astype(F32)
    )
    for c in (c1, c2, c3, c4, c5, c6):
        c.wait_send()
    return total


def layer_kernel(
    rates,
    docs,
    q_ref,
    k_ref,
    v_ref,
    routes_t,
    router_t,
    res_hbm,
    wo_hbm,
    gate_hbm,
    up_hbm,
    down_hbm,
    out_ref,
    *scratch,
):
    (
        (wo, res, st_send, st_recv, ca_send, ca_recv, coef, inside, attn, kept),
        (p_ref, relay, acc, got, relay2, acc2, got2),
        (nbuf, wgu, wd, pick, ones, hit, slots, mixw, x, hbuf, abuf, y, y_recv, back, z_recv, table),
        (alsem, as1, ar1, as2, ar2, as3, ar3, as4, ar4),
        (lsem, s1, r1, sz, rz, s2, r2, s3, r3, sq, rq, s4, r4, s5, r5),
    ) = jax.tree.unflatten(SCRATCH_TREE, scratch)
    me, z = lax.axis_index("seq"), lax.axis_index("exp")
    chip, core = me // 2, lax.rem(me, 2)
    other = 1 - core
    cx, cy = chip // 4, lax.rem(chip, 4)
    partner = (chip * 2 + other, z)
    up_z, down_z = lax.rem(z + 1, NZ), lax.rem(z + 3, NZ)
    parity, level = lax.rem(z, 2), z // 2
    barrier = entry_signal(me, z)
    load_wo = pltpu.make_async_copy(wo_hbm, wo, alsem.at[0])
    load_wo.start()
    load_res = pltpu.make_async_copy(res_hbm.at[rows(z, OWN), :], res, alsem.at[1])
    load_res.start()
    load_g = pltpu.make_async_copy(gate_hbm.at[0], wgu.at[:, 0:SL], lsem.at[1])
    load_u = pltpu.make_async_copy(up_hbm.at[0], wgu.at[:, SL : 2 * SL], lsem.at[2])
    load_d = pltpu.make_async_copy(down_hbm.at[0], wd, lsem.at[3])
    for c in (load_g, load_u, load_d):
        c.start()

    starts = [jnp.int32(0)]
    for i in range(15):
        starts.append(starts[-1] + docs[i])

    def doc_at(pos):
        total = jnp.zeros(pos.shape, I32)
        for s in starts:
            total = total + (pos >= s).astype(I32)
        return total

    base = me * TOK
    t_col = lax.broadcasted_iota(I32, (TOK, 1), 0)
    t_row = lax.broadcasted_iota(I32, (1, TOK), 1)
    doc_col = doc_at(base + t_col)
    doc_row = doc_at(base + t_row)
    doc_first, doc_last = jnp.int32(0), jnp.int32(0)
    for s in starts:
        doc_first = doc_first + (base >= s).astype(I32)
        doc_last = doc_last + (base + TOK - 1 >= s).astype(I32)
    same_last = (doc_col == doc_last).astype(F32)
    same_first = (doc_col == doc_first).astype(F32)
    end_dist = (TOK - t_col).astype(F32)
    local_f = t_col.astype(F32)

    for h in range(HEADS):
        cols = slice(h * HS, (h + 1) * HS)
        w = jnp.exp(-rates[h] * end_dist) * same_last
        kw = (k_ref[:, cols].astype(F32) * w).astype(BF16)
        state = lax.dot_general(
            kw, v_ref[:, cols], (((0,), (0,)), ((), ())), preferred_element_type=F32
        )
        st_send[h * HS : (h + 1) * HS, :] = state.astype(BF16)

    entry_wait(barrier)
    own_st = pltpu.make_async_copy(st_send.at[rows(me, 32), :], st_recv.at[me], alsem.at[2])
    own_st.start()

    def send_state(d):
        j = lax.rem(me + d, NSEQ)
        return rcopy(
            st_send.at[rows(j, 32), :], st_recv.at[me], as1.at[d], ar1.at[me], (j, z)
        )

    @pl.loop(1, NSEQ)
    def _(d):
        send_state(d).start()

    lag = lax.broadcasted_iota(I32, (TOK, TOK), 0) - lax.broadcasted_iota(I32, (TOK, TOK), 1)
    allowed = (lag >= 0) & (doc_col == doc_row)
    lag_f = jnp.where(allowed, lag.astype(F32), 3e38)

    def inner(h):
        cols = slice(h * HS, (h + 1) * HS)
        scores = lax.dot_general(
            q_ref[:, cols], k_ref[:, cols], (((1,), (1,)), ((), ())), preferred_element_type=F32
        )
        probs = (scores * jnp.exp(-rates[h] * lag_f)).astype(BF16)
        inside[h] = jnp.dot(probs, v_ref[:, cols], preferred_element_type=F32)

    for h in range(6):
        inner(h)

    own_st.wait()

    @pl.loop(1, NSEQ)
    def _(d):
        j = lax.rem(me + d, NSEQ)
        rcopy(st_send.at[rows(j, 32), :], st_recv.at[j], as1.at[d], ar1.at[j], (j, z)).wait_recv()

    c_pos = lax.broadcasted_iota(I32, (NSEQ, HS), 0) * TOK
    d_here = doc_at(c_pos)
    u = (d_here == doc_at(c_pos - 1)).astype(F32)
    g = (d_here == doc_at(c_pos - TOK)).astype(F32)
    r_own = rates[me // (NSEQ // HEADS)]
    coef[0] = u
    coef[1] = g * jnp.exp(jnp.full((NSEQ, HS), -float(TOK), F32) * r_own)
    total = jnp.zeros((32, HS), F32)
    ca_send[0] = total.astype(BF16)
    for c in range(1, NSEQ):
        total = coef[1, c : c + 1, :] * total + coef[0, c : c + 1, :] * st_recv[c - 1].astype(F32)
        ca_send[c] = total.astype(BF16)

    own_ca = pltpu.make_async_copy(ca_send.at[me], ca_recv.at[me], alsem.at[3])
    own_ca.start()

    @pl.loop(1, NSEQ)
    def _(d):
        j = lax.rem(me + d, NSEQ)
        rcopy(ca_send.at[j], ca_recv.at[me], as2.at[d], ar2.at[me], (j, z)).start()

    for h in range(6, 8):
        inner(h)

    def rank_wanted(shape, axis):
        r = lax.broadcasted_iota(I32, shape, axis)
        return (parity * 8 + lax.rem(r // 8, 2) * 16 + lax.rem(r, 8)).astype(F32)

    def onehot(flag):
        return flag.astype(F32).astype(BF16)

    def flip(a):
        return lax.dot_general(a, eye, (((0,), (0,)), ((), ())), preferred_element_type=F32)

    e_sub = lax.broadcasted_iota(I32, (16, TOK), 0)
    one0_t = onehot(routes_t[0:1, :] == e_sub)
    one1_t = onehot(routes_t[1:2, :] == e_sub)
    chosen_t = one0_t + one1_t
    before_t = onehot(
        lax.broadcasted_iota(I32, (TOK, TOK), 0) < lax.broadcasted_iota(I32, (TOK, TOK), 1)
    )
    rank_t = jnp.dot(chosen_t, before_t, preferred_element_type=F32).astype(BF16)
    expand_t = onehot(
        lax.broadcasted_iota(I32, (TOK, 16), 0) // 16 == lax.broadcasted_iota(I32, (TOK, 16), 1)
    )
    rank_big = jnp.dot(expand_t, rank_t, preferred_element_type=F32)
    chosen_big = jnp.dot(expand_t, chosen_t, preferred_element_type=F32)
    pick[...] = jnp.where(rank_big == rank_wanted((TOK, 1), 0), chosen_big, 0.0).astype(BF16)
    eye = onehot(
        lax.broadcasted_iota(I32, (16, 16), 0) == lax.broadcasted_iota(I32, (16, 16), 1)
    )
    ones[0] = flip(one0_t)
    ones[1] = flip(one1_t)
    expand = onehot(
        lax.broadcasted_iota(I32, (16, TOK), 1) // 16 == lax.broadcasted_iota(I32, (16, TOK), 0)
    )
    rank_w = jnp.dot(flip(rank_t).astype(BF16), expand, preferred_element_type=F32)
    hit[...] = (rank_w == rank_wanted((1, TOK), 1)).astype(F32)

    own_ca.wait()

    @pl.loop(1, NSEQ)
    def _(d):
        j = lax.rem(me + d, NSEQ)
        rcopy(ca_send.at[j], ca_recv.at[j], as2.at[d], ar2.at[j], (j, z)).wait_recv()

    for h in range(HEADS):
        cols = slice(h * HS, (h + 1) * HS)
        carried = ca_recv[h * 4 : (h + 1) * 4].reshape(HS, HS)
        term = jnp.dot(q_ref[:, cols], carried, preferred_element_type=F32)
        raw = inside[h] + term * (jnp.exp(-rates[h] * local_f) * same_first)
        scale = lax.rsqrt(jnp.mean(raw * raw, axis=-1, keepdims=True) + EPSILON)
        attn[:, cols] = (raw * scale).astype(BF16)

    load_wo.wait()

    def project(h):
        p_ref[:, HALVES[h]] = jnp.dot(
            attn[...], wo[:, HALVES[h]], preferred_element_type=F32
        ).astype(BF16)

    right, left, far = lax.rem(z + 1, NZ), lax.rem(z + 3, NZ), lax.rem(z + 2, NZ)
    dr, dl = (me, right), (me, left)

    def quarters(h):
        return (
            slice(h * HALF, h * HALF + QUART),
            slice(h * HALF + QUART, (h + 1) * HALF),
        )

    def rs(h):
        qa, qb = quarters(h)

        def go(j, src, dst, dev):
            return rcopy(src, dst, as3.at[h, j], ar3.at[h, j], dev)

        return (
            go(0, p_ref.at[rows(far, OWN), qa], relay.at[h, 0], dr),
            go(1, p_ref.at[rows(far, OWN), qb], relay.at[h, 1], dl),
            go(2, p_ref.at[rows(right, OWN), qb], got.at[0, :, qb], dr),
            go(3, p_ref.at[rows(left, OWN), qa], got.at[1, :, qa], dl),
            go(4, acc.at[h, 0], got.at[0, :, qa], dr),
            go(5, acc.at[h, 1], got.at[1, :, qb], dl),
        )

    def ag(h):
        qa, qb = quarters(h)

        def go(j, owner, cols, dev):
            view = nbuf.at[rows(owner, OWN), cols]
            return rcopy(view, view, as4.at[h, j], ar4.at[h, j], dev)

        return (
            go(0, z, qa, dr),
            go(1, z, qb, dl),
            go(2, z, qb, dr),
            go(3, z, qa, dl),
            go(4, left, qa, dr),
            go(5, right, qb, dl),
        )

    def first_sends(c):
        for j in (0, 3, 1, 2):
            c[j].start()

    def rs_relay(h):
        qa, qb = quarters(h)
        c = rs_copies[h]
        c[0].wait_recv()
        acc[h, 0] = (
            p_ref[rows(right, OWN), qa].astype(F32) + relay[h, 0].astype(F32)
        ).astype(BF16)
        c[4].start()
        c[1].wait_recv()
        acc[h, 1] = (p_ref[rows(left, OWN), qb].astype(F32) + relay[h, 1].astype(F32)).astype(BF16)
        c[5].start()

    def rs_end(h):
        for j in (2, 3, 4, 5):
            rs_copies[h][j].wait_recv()
        cols = HALVES[h]
        share = (
            p_ref[rows(z, OWN), cols].astype(F32)
            + got[0, :, cols].astype(F32)
            + got[1, :, cols].astype(F32)
        )
        hidden = (res[:, cols].astype(F32) + share).astype(BF16)
        kept[:, cols] = hidden
        nbuf[rows(z, OWN), cols] = hidden
        first_sends(ag_copies[h])

    def ag_relay(h):
        c = ag_copies[h]
        c[0].wait_recv()
        c[4].start()
        c[1].wait_recv()
        c[5].start()

    def ag_end(h):
        for j in (2, 3, 4, 5):
            ag_copies[h][j].wait_recv()

    def squares(h):
        part = nbuf[:, HALVES[h]].astype(F32)
        return jnp.sum(part * part, axis=-1, keepdims=True)

    rs_copies, ag_copies = (rs(0), rs(1)), (ag(0), ag(1))
    project(0)
    first_sends(rs_copies[0])
    project(1)
    rs_relay(0)
    first_sends(rs_copies[1])
    load_res.wait()
    rs_end(0)
    rs_relay(1)
    ag_relay(0)
    rs_end(1)
    ag_end(0)

    def away(i, sign):
        m = lax.rem(i, 4)
        dx = lax.rem(2 * m, 4) + m // 2
        dy = lax.rem(i // 4 - dx + 4, 4)
        return lax.rem(cx + sign * dx + 4, 4) * 4 + lax.rem(cy + sign * dy + 4, 4)

    def span(start, size, align):
        return pl.ds(pl.multiple_of(start, align), size)

    def x_rows(st, i):
        i0, n = st
        return span(64 * i0 + core * 32 * n + parity * 16 * n + (i - i0) * 16, 16, 16)

    def x_unit(st, i, unit):
        i0, n = st
        r = 64 * i0 + core * 32 * n + lax.rem(unit, 2) * 16 * n + (i - i0) * 16
        return span(r + (unit // 2) * 8, 8, 8)

    def half(st, par):
        i0, n = st
        return span(64 * i0 + par * 32 * n, 32 * n, 32 * n)

    def b_all(st):
        i0, n = st
        return pl.ds(32 * i0, 32 * n)

    def b_rows(st, i):
        i0, n = st
        return span(32 * i0 + parity * 16 * n + (i - i0) * 16, 16, 16)

    def b_unit(st, i, unit):
        i0, n = st
        r = 32 * i0 + lax.rem(unit, 2) * 16 * n + (i - i0) * 16
        return span(r + (unit // 2) * 8, 8, 8)

    def loop_over(st, fn, skip=0):
        i0, n = st

        @pl.loop(i0 + skip, i0 + n)
        def _(i):
            fn(i)

    def send1(st, i, h):
        e = away(i, 1)
        return rcopy(
            slots.at[rows(e, 16), XC[h]],
            x.at[x_rows(st, i), XC[h]],
            s1.at[i, h],
            r1.at[i, h],
            (e * 2 + core, z),
        )

    def keep1(h):
        return pltpu.make_async_copy(
            slots.at[rows(chip, 16), XC[h]],
            x.at[x_rows(STAGES[0], 0), XC[h]],
            lsem.at[7 + h],
        )

    def dispatch(h):
        slots[:, XC[h]] = jnp.dot(
            pick[...], nbuf[:, XC[h]], preferred_element_type=F32
        ).astype(BF16)
        keep1(h).start()
        for st in STAGES:
            loop_over(st, lambda i: send1(st, i, h).start(), 1 if st[0] == 0 else 0)

    dispatch(0)
    square_sum = squares(0)
    ag_relay(1)
    ag_end(1)
    scale = lax.rsqrt((square_sum + squares(1)) * (1.0 / D) + EPSILON)
    high = scale.astype(BF16).astype(F32)
    lane = lax.broadcasted_iota(I32, (TOK, 128), 1)
    nbuf[:, D:WIDE] = jnp.where(
        lane == 0, high, jnp.where(lane == 1, scale - high, 0.0)
    ).astype(BF16)
    dispatch(1)

    for c in (load_g, load_u, load_d):
        c.wait()

    def pass_on(st, i, side, h):
        view = x.at[x_unit(st, i, z), XC[h]]
        to = up_z if side == 0 else down_z
        return rcopy(view, view, sz.at[i, side, h], rz.at[i, side, h], (me, to))

    def passed(st, i, side, h):
        view = x.at[x_unit(st, i, down_z if side == 0 else up_z), XC[h]]
        return rcopy(view, view, sz.at[i, side, h], rz.at[i, side, h], (me, up_z))

    def arrive(k, h):
        st = STAGES[k]
        skip = 1 if st[0] == 0 else 0
        if skip:
            keep1(h).wait()
            pass_on(st, 0, 0, h).start()
            pass_on(st, 0, 1, h).start()

        def one(i):
            view = x.at[x_rows(st, i), XC[h]]
            rcopy(view, view, s1.at[0, 0], r1.at[i, h], partner).wait_recv()
            pass_on(st, i, 0, h).start()
            pass_on(st, i, 1, h).start()

        loop_over(st, one, skip)

    def hand(k, side, h):
        view = x.at[half(STAGES[k], side), XC[h]]
        return rcopy(view, view, s2.at[k, h], r2.at[k, h], partner)

    def hand_over(k, h):
        def one(i):
            passed(STAGES[k], i, 0, h).wait_recv()
            passed(STAGES[k], i, 1, h).wait_recv()

        loop_over(STAGES[k], one)
        hand(k, core, h).start()

    def pair(k, h):
        st = STAGES[k]
        return rcopy(
            y.at[half(st, other), HALVES[h]],
            y_recv.at[b_all(st), HALVES[h]],
            s3.at[k, h],
            r3.at[k, h],
            partner,
        )

    def z_back(st, i, side, h):
        unit = up_z if side == 0 else down_z
        return rcopy(
            back.at[b_unit(st, i, unit), HALVES[h]],
            z_recv.at[side, rows(i, 8), HALVES[h]],
            sq.at[i, side, h],
            rq.at[i, side, h],
            (me, unit),
        )

    def pair_sum(k, h):
        st, cols = STAGES[k], HALVES[h]
        pair(k, h).wait_recv()
        back[b_all(st), cols] = (
            y[half(st, core), cols].astype(F32) + y_recv[b_all(st), cols].astype(F32)
        ).astype(BF16)

        def one(i):
            z_back(st, i, 0, h).start()
            z_back(st, i, 1, h).start()

        loop_over(st, one)

    def send_back(st, i, h):
        return rcopy(
            back.at[b_rows(st, i), HALVES[h]],
            table.at[rows(chip, 16), HALVES[h]],
            s4.at[i, h],
            r4.at[i, h],
            (away(i, -1) * 2 + core, z),
        )

    def stay(h):
        return pltpu.make_async_copy(
            back.at[b_rows(STAGES[0], 0), HALVES[h]],
            table.at[rows(chip, 16), HALVES[h]],
            lsem.at[5 + h],
        )

    def z_sum(k, h):
        st, cols = STAGES[k], HALVES[h]

        def one(i):
            z_back(st, i, 0, h).wait_recv()
            z_back(st, i, 1, h).wait_recv()
            r = b_unit(st, i, z)
            back[r, cols] = (
                back[r, cols].astype(F32)
                + z_recv[0, rows(i, 8), cols].astype(F32)
                + z_recv[1, rows(i, 8), cols].astype(F32)
            ).astype(BF16)

        loop_over(st, one)
        skip = 1 if st[0] == 0 else 0
        if skip:
            stay(h).start()
        loop_over(st, lambda i: send_back(st, i, h).start(), skip)

    last = len(STAGES) - 1

    def first_half(k):
        hand(k, other, 0).wait_recv()
        r = slice(256 * k, 256 * (k + 1))
        hbuf[r, :] = jnp.dot(x[r, XC[0]], wgu[0:HALF, :], preferred_element_type=F32)

    arrive(0, 0)
    arrive(1, 0)
    arrive(2, 0)
    hand_over(0, 0)
    arrive(3, 0)
    hand_over(1, 0)
    first_half(0)
    arrive(0, 1)
    hand_over(2, 0)
    first_half(1)
    arrive(1, 1)
    hand_over(3, 0)
    first_half(2)

    logits = scale * lax.dot_general(
        nbuf[:, 0:D], router_t[...], (((1,), (1,)), ((), ())), preferred_element_type=F32
    )
    one0, one1 = ones[0], ones[1]
    l0 = jnp.sum(one0 * logits, axis=1, keepdims=True)
    l1 = jnp.sum(one1 * logits, axis=1, keepdims=True)
    weight = one0 * jax.nn.sigmoid(l0 - l1) + one1 * jax.nn.sigmoid(l1 - l0)
    expand = onehot(
        lax.broadcasted_iota(I32, (16, TOK), 1) // 16 == lax.broadcasted_iota(I32, (16, TOK), 0)
    )
    weight_w = jnp.dot(weight.astype(BF16), expand, preferred_element_type=F32)
    mixw[...] = (weight_w * hit[...]).astype(BF16)

    hand_over(0, 1)
    first_half(3)
    for k, (i0, n) in enumerate(STAGES):
        m = 64 * n
        r = slice(64 * i0, 64 * i0 + m)
        hand(k, other, 1).wait_recv()
        hbuf[r, :] += jnp.dot(x[r, HALF:D], wgu[HALF:D, :], preferred_element_type=F32)
        if k < last:
            hand_over(k + 1, 1)
        if k + 1 < last:
            arrive(k + 2, 1)
        if k > 0:
            pair_sum(k - 1, 0)
            pair_sum(k - 1, 1)
        parts = x[r, D:WIDE].astype(F32)
        row_scale = parts[:, 0:1] + parts[:, 1:2]
        gate, up = hbuf[r, 0:SL] * row_scale, hbuf[r, SL : 2 * SL] * row_scale
        abuf[0:m, :] = (gate * jax.nn.sigmoid(gate) * up).astype(BF16)
        for h in (0, 1):
            y[64 * i0 : 64 * i0 + m, HALVES[h]] = jnp.dot(
                abuf[0:m, :], wd[:, HALVES[h]], preferred_element_type=F32
            ).astype(BF16)
            pair(k, h).start()
            if k > 1:
                z_sum(k - 2, h)

    for h in (0, 1):
        for c in (*rs_copies[h], *ag_copies[h]):
            c.wait_send()

    pair_sum(last, 0)
    pair_sum(last, 1)
    z_sum(last - 1, 0)
    z_sum(last - 1, 1)
    z_sum(last, 0)
    z_sum(last, 1)

    def mix(h):
        stay(h).wait()

        @pl.loop(1, 16)
        def _(i):
            view = table.at[rows(away(i, 1), 16), HALVES[h]]
            rcopy(view, view, s4.at[0, 0], r4.at[i, h], partner).wait_recv()

        p_ref[:, HALVES[h]] = jnp.dot(
            mixw[...], table[:, HALVES[h]], preferred_element_type=F32
        ).astype(BF16)

    share = reduce_scatter_z(me, z, mix, p_ref, relay2, acc2, got2, s5, r5)
    out_ref[...] = (kept[...].astype(F32) + share).astype(BF16)

    for k, st in enumerate(STAGES):
        hand(k, core, 0).wait_send()
        hand(k, core, 1).wait_send()
        pair(k, 0).wait_send()
        pair(k, 1).wait_send()
        skip = 1 if st[0] == 0 else 0

        def one(i):
            send1(st, i, 0).wait_send()
            send1(st, i, 1).wait_send()
            send_back(st, i, 0).wait_send()
            send_back(st, i, 1).wait_send()

        loop_over(st, one, skip)

        def two(i):
            for side in (0, 1):
                pass_on(st, i, side, 0).wait_send()
                pass_on(st, i, side, 1).wait_send()
                z_back(st, i, side, 0).wait_send()
                z_back(st, i, side, 1).wait_send()

        loop_over(st, two)

    @pl.loop(1, NSEQ)
    def _(d):
        j = lax.rem(me + d, NSEQ)
        send_state(d).wait_send()
        rcopy(ca_send.at[j], ca_recv.at[me], as2.at[d], ar2.at[me], (j, z)).wait_send()


VM = pl.BlockSpec(memory_space=pltpu.VMEM)
SM = pl.BlockSpec(memory_space=pltpu.SMEM)
HB = pl.BlockSpec(memory_space=pl.ANY)
DMA = pltpu.SemaphoreType.DMA
V = pltpu.VMEM

SCRATCH = (
    (
        V((HEADS * HS, D), BF16),
        V((OWN, D), BF16),
        V((HEADS * HS, HS), BF16),
        V((NSEQ, 32, HS), BF16),
        V((NSEQ, 32, HS), BF16),
        V((NSEQ, 32, HS), BF16),
        V((2, NSEQ, HS), F32),
        V((HEADS, TOK, HS), F32),
        V((TOK, HEADS * HS), BF16),
        V((OWN, D), BF16),
    ),
    (
        V((TOK, D), BF16),
        V((2, 2, OWN, QUART), BF16),
        V((2, 2, OWN, QUART), BF16),
        V((2, OWN, D), BF16),
        V((2, OWN, HALF), BF16),
        V((2, OWN, HALF), BF16),
        V((2, OWN, D), BF16),
    ),
    (
        V((TOK, WIDE), BF16),
        V((D, 2 * SL), BF16),
        V((SL, D), BF16),
        V((TOK, TOK), BF16),
        V((2, TOK, 16), F32),
        V((TOK, TOK), F32),
        V((TOK, WIDE), BF16),
        V((TOK, TOK), BF16),
        V((4 * TOK, WIDE), BF16),
        V((4 * TOK, 2 * SL), F32),
        V((TOK, SL), BF16),
        V((4 * TOK, D), BF16),
        V((2 * TOK, D), BF16),
        V((2 * TOK, D), BF16),
        V((2, 128, D), BF16),
        V((TOK, D), BF16),
    ),
    tuple(DMA((n,)) for n in (5, NSEQ, NSEQ, NSEQ, NSEQ)) + tuple(DMA((2, 6)) for _ in range(4)),
    (
        DMA((9,)),
        DMA((16, 2)),
        DMA((16, 2)),
        DMA((16, 2, 2)),
        DMA((16, 2, 2)),
        DMA((len(STAGES), 2)),
        DMA((len(STAGES), 2)),
        DMA((len(STAGES), 2)),
        DMA((len(STAGES), 2)),
        DMA((16, 2, 2)),
        DMA((16, 2, 2)),
        DMA((16, 2)),
        DMA((16, 2)),
        DMA((6,)),
        DMA((6,)),
    ),
)
SCRATCH_LIST, SCRATCH_TREE = jax.tree.flatten(SCRATCH)


def body(
    residual_in,
    queries,
    keys,
    values,
    rates,
    doc_lengths,
    out_weight,
    router,
    gate_weight,
    up_weight,
    down_weight,
    routes,
):
    return pl.pallas_call(
        layer_kernel,
        name="layer",
        out_shape=jax.ShapeDtypeStruct((OWN, D), BF16),
        in_specs=[SM, SM, VM, VM, VM, VM, VM, HB, HB, HB, HB, HB],
        out_specs=VM,
        scratch_shapes=SCRATCH_LIST,
        compiler_params=pltpu.CompilerParams(
            collective_id=0, has_side_effects=True, vmem_limit_bytes=VMEM_LIMIT
        ),
    )(
        rates,
        doc_lengths,
        queries,
        keys,
        values,
        routes.T,
        router.T,
        residual_in,
        out_weight,
        gate_weight,
        up_weight,
        down_weight,
    )


def solution(mesh):
    in_specs = (
        P("seq", None),
        P("seq", "exp"),
        P("seq", "exp"),
        P("seq", "exp"),
        P("exp"),
        P(),
        P("exp", None),
        P(),
        P("seq", None, "exp"),
        P("seq", None, "exp"),
        P("seq", "exp", None),
        P("seq", None),
    )
    out_specs = P(("seq", "exp"), None)
    return jax.shard_map(body, mesh=mesh, in_specs=in_specs, out_specs=out_specs, check_vma=False)
```
